128 devices in a mesh: leaf: 32 (over x, z, core), level: 4 (over y).
Axes of the slice: x: 4, y: 4, z: 4, core: 2. Of those that a mesh axis runs over, the one named last changes fastest.
Arguments:
- right_side: float32 [8, 2097152], P(None, ('leaf', 'level')), may hold values from -28 to 28
- basis: bfloat16 [16384, 128, 128], P(('leaf', 'level')), may hold values from -0.5 to 0.5
- transfer: bfloat16 [16384, 128, 128], P(('leaf', 'level')), may hold values from -0.5 to 0.5
- order: int32 [128, 128], P(('leaf', 'level')), may hold values from 0 to 127, each once within a row
- far_src: int32 [4096, 4], P(('leaf', 'level')), may hold values from 0 to 127
- far_mats: bfloat16 [4096, 4, 128, 128], P(('leaf', 'level')), may hold values from -0.125 to 0.125
- near_target: int32 [32768], P(('leaf', 'level')), may hold values from 0 to 127
- near_dest: int32 [32768, 1], P(('leaf', 'level')), may hold values from 0 to 127; in each aligned block of 256 rows (0 to 255, 256 to 511, ...) at most 4 rows name the same one
- near_src: int32 [32768], P(('leaf', 'level')), may hold values from 0 to 127
- near_blocks: bfloat16 [32768, 128, 128], P(('leaf', 'level')), may hold values from -0.5 to 0.5
Outputs:
- solution: float32 [8, 2097152], P(None, ('leaf', 'level'))
- residual: float32 [8, 2097152], P(None, ('leaf', 'level'))
The draws below stay inside these ranges and needn't reach their ends.
Inputs may be any that keep to these rules, and one draw needn't show every extreme that they name: `order`: each group's row is a permutation of 0 to 127. `near_dest`: among the pairs of one group, no group is named more than 4 times, a bound that some block reaches.
All inputs are finite; a program needn't handle non-finite values.
Results may differ from the reference program's by a relative error of at most 0.0022.
Values may be sent and summed in bfloat16 or wider, within the bound.
A program may use at most 128 MiB of HBM per device.

```python
import math
import jax
import jax.numpy as jnp
import numpy as np
from jax import lax

POINTS = 128
COEFFS = 128
SYSTEMS = 8
CLUSTER_DEV = 128
CHILDREN = 4
FAR_PARTNERS = 4
NEAR_DEV = 256
GROUPS = 128
CAPACITY = 4
LEVELS = 4
PARENT_DEV = 32
PER_PEER = 1
TABLE_ROWS = 128
CLUSTERS = 16384
PANELS = 2097152
PARENTS = 4096
NEAR_PAIRS = 32768


def draw_right_side(key, part):
    key_base, key_cols, key_rows = jax.random.split(key, 3)
    position = jnp.arange(PANELS, dtype=jnp.float32) / PANELS
    gradient = jnp.exp((position - 0.5) * math.log(3.0))[None, :]
    col_scale = jnp.exp(jax.random.uniform(key_cols, (1, PANELS), jnp.float32, -1.15, 1.15))
    row_scale = jnp.exp(jax.random.uniform(key_rows, (SYSTEMS, 1), jnp.float32, -1.15, 1.15))
    base_draw = jnp.clip(jax.random.normal(key_base, (SYSTEMS, PANELS), jnp.float32), -4.0, 4.0)
    return base_draw * gradient * col_scale * row_scale * 0.4


def plant(result, stream_key, smallest, largest):
    spot = [jax.random.randint(jax.random.fold_in(stream_key, axis), (), 0, length) for axis, length in enumerate(result.shape)]
    longest = result.shape.index(max(result.shape))
    beside = spot[:longest] + [(spot[longest] + 1) % result.shape[longest]] + spot[longest + 1:]
    return result.at[tuple(spot)].set(smallest).at[tuple(beside)].set(largest)


def level_of(rng, extent, pieces, smallest, top_value):
    loudness, own = 1.0, jax.random.fold_in(rng, 6)
    for dim, shards_of in pieces:
        draws = jnp.exp(jax.random.uniform(jax.random.fold_in(own, dim), (shards_of,), jnp.float32, smallest / len(pieces), top_value / len(pieces)))
        loudness = loudness * jnp.repeat(draws, extent[dim] // shards_of).reshape([-1 if axis == dim else 1 for axis in range(len(extent))])
    return loudness


def routed_block(key, own, number, rows, number_of, top, bound, lean):
    ranking = jax.random.permutation(key, number_of)
    crowded, ordinary = shares(number_of, rows * top, bound, lean, True), shares(number_of, rows * top, bound, lean, False)
    places = jnp.arange(number_of)

    def named(sizes, offset_by):
        used = int((sizes > 0).sum())
        fixed = max(1, used // 4)
        shifted = fixed + (places - fixed + offset_by * (used - fixed)) % max(1, number_of - fixed)
        return jnp.zeros((number_of,), jnp.int32).at[ranking[jnp.where(places < fixed, places, shifted)]].set(jnp.asarray(sizes, jnp.int32))

    sizes = jnp.where(number % 4 == 0, named(crowded, number // 4), named(ordinary, number - number // 4 - 1))
    mixed = jax.random.permutation(jax.random.fold_in(own, 3), number_of)
    donor, sink = mixed[0:number_of // 2 * 2:2], mixed[1:number_of // 2 * 2:2]
    slack = jnp.minimum(sizes[donor] - 1, bound - sizes[sink]) // 2
    slack = jnp.where((donor == ranking[0]) | (sink == ranking[0]) | (sizes[sink] == 0), 0, jnp.maximum(slack, 0))
    shifted = jax.random.randint(jax.random.fold_in(own, 4), (number_of // 2,), 0, 1 << 20) % (slack + 1)
    sizes = sizes.at[donor].add(-shifted).at[sink].add(shifted)
    labels = jnp.searchsorted(jnp.cumsum(sizes), jnp.arange(rows * top), side="right").astype(jnp.int32)
    table = labels.reshape(top, rows).T
    table = table[jax.random.permutation(jax.random.fold_in(own, 1), rows)]
    offset_by = jax.random.randint(jax.random.fold_in(own, 2), (rows, 1), 0, top)
    return jnp.take_along_axis(table, (jnp.arange(top)[None, :] + offset_by) % top, axis=1)


def shares(number_of, total, limit, lean, full):
    portions = [(1 << 20) // math.isqrt(standing ** lean) + 1 for standing in range(1, number_of + 1)]
    largest = limit if full else min(limit, max(-(-total // number_of), total * portions[0] // sum(portions)))
    least = 1 if total - largest >= number_of - 1 else 0
    counts, rest = [largest] + [least] * (number_of - 1), total - largest - least * (number_of - 1)
    while rest > 0:
        free = [i for i in range(1, number_of) if counts[i] < largest] or [i for i in range(1, number_of) if counts[i] < limit]
        whole, remaining = sum([portions[i] for i in free]), rest
        for i in free:
            more = min(limit - counts[i], max(1, remaining * portions[i] // whole), rest)
            counts[i] = counts[i] + more
            rest = rest - more
    return np.array(counts)


def gaussian(rng, dims, scale, most, cuts=(), kind=jnp.bfloat16):
    values = jax.random.normal(rng, dims, jnp.float32) * scale
    if len(cuts) > 0:
        values = level_of(rng, dims, cuts, -0.22, 0.18) * values
    return jnp.clip(values, min=-most, max=most).astype(kind)


def setup_inputs(seed: int = 0) -> dict:
    key_of = jax.random.split(jax.random.key(seed), 11)
    right_side = draw_right_side(jax.random.fold_in(key_of[10], 71), 0)
    basis = gaussian(key_of[1], (CLUSTERS, POINTS, COEFFS), POINTS ** -0.5, 0.5, ((0, 128),))
    transfer = gaussian(key_of[2], (CLUSTERS, COEFFS, COEFFS), COEFFS ** -0.5, 0.5, ((0, 128),))
    order = jax.vmap(lambda own: jax.random.permutation(own, CLUSTER_DEV))(jax.random.split(key_of[3], GROUPS)).reshape((GROUPS, CLUSTER_DEV)).astype(jnp.int32)
    far_src = plant(jax.random.randint(key_of[4], (PARENTS, FAR_PARTNERS), 0, TABLE_ROWS), jax.random.fold_in(key_of[4], 1), 0, TABLE_ROWS - 1).astype(jnp.int32)
    far_mats = gaussian(key_of[5], (PARENTS, FAR_PARTNERS, COEFFS, COEFFS), (COEFFS * FAR_PARTNERS * CHILDREN) ** -0.5, 0.125, ((0, 128),))
    near_target = plant(jax.random.randint(key_of[6], (NEAR_PAIRS,), 0, CLUSTER_DEV), jax.random.fold_in(key_of[6], 1), 0, CLUSTER_DEV - 1).astype(jnp.int32)
    near_dest_keys = jax.random.split(jax.random.fold_in(key_of[7], 1), NEAR_PAIRS // NEAR_DEV)
    near_dest_turns = jax.random.permutation(jax.random.fold_in(key_of[7], 3), NEAR_PAIRS // NEAR_DEV)
    near_dest = jax.vmap(lambda own, number: routed_block(jax.random.fold_in(key_of[7], 2), own, number, NEAR_DEV, GROUPS, 1, CAPACITY, 2))(near_dest_keys, near_dest_turns).reshape((NEAR_PAIRS, 1))
    near_src = plant(jax.random.randint(key_of[8], (NEAR_PAIRS,), 0, CLUSTER_DEV), jax.random.fold_in(key_of[8], 1), 0, CLUSTER_DEV - 1).astype(jnp.int32)
    near_blocks = gaussian(key_of[9], (NEAR_PAIRS, POINTS, POINTS), POINTS ** -0.5, 0.5, ((0, 128),))
    return {"right_side": right_side, "basis": basis, "transfer": transfer, "order": order, "far_src": far_src, "far_mats": far_mats, "near_target": near_target, "near_dest": near_dest, "near_src": near_src, "near_blocks": near_blocks}


EPSILON = 1e-06

def narrow(values):
    return lax.optimization_barrier(values.astype(jnp.bfloat16)).astype(jnp.float32)

def operator(vector_in, basis, transfer, order, far_src, far_mats, near_target, near_dest, near_src, near_blocks):
    rounded = narrow(vector_in).reshape(SYSTEMS, GROUPS, CLUSTER_DEV, POINTS)
    target_rows = near_target.reshape(GROUPS, NEAR_DEV)
    dest_rows = near_dest.reshape(GROUPS, NEAR_DEV)
    source_rows = near_src.reshape(GROUPS, NEAR_DEV)
    block_rows = near_blocks.reshape(GROUPS, NEAR_DEV, POINTS, POINTS)
    group_ids = jnp.arange(GROUPS, dtype=jnp.int32)

    def near_step(total, group):
        gathered = rounded[:, group][:, target_rows[group]]
        partial_rows = jnp.einsum('rnp,npq->rnq', gathered, block_rows[group].astype(jnp.float32))
        return (total.at[:, dest_rows[group], source_rows[group]].add(partial_rows), None)
    near_sum, _ = lax.scan(near_step, jnp.zeros((SYSTEMS, GROUPS, CLUSTER_DEV, POINTS), jnp.float32), group_ids)
    basis_rows = basis.reshape(GROUPS, CLUSTER_DEV, POINTS, COEFFS)
    transfer_rows = transfer.reshape(GROUPS, CLUSTER_DEV, COEFFS, COEFFS)

    def up_step(group):
        perm_row = order[group]
        ordered = rounded[:, group][:, perm_row]
        expansion = narrow(jnp.einsum('rsp,spk->srk', ordered, basis_rows[group][perm_row].astype(jnp.float32)))
        return jnp.einsum('srk,skj->srj', expansion, transfer_rows[group][perm_row].astype(jnp.float32))
    lifted = lax.map(up_step, group_ids)
    arrived = lifted.reshape(GROUPS, GROUPS, PER_PEER, SYSTEMS, COEFFS).transpose(1, 0, 2, 3, 4)
    arrived = arrived.reshape(GROUPS, CLUSTER_DEV, SYSTEMS, COEFFS)
    parent = narrow(lax.optimization_barrier(jnp.sum(arrived.reshape(GROUPS, PARENT_DEV, CHILDREN, SYSTEMS, COEFFS), axis=2)))
    parent_table = parent.reshape(GROUPS // LEVELS, TABLE_ROWS, SYSTEMS, COEFFS)
    far_rows = far_src.reshape(GROUPS, PARENT_DEV * FAR_PARTNERS)
    far_blocks = far_mats.reshape(GROUPS, PARENT_DEV, FAR_PARTNERS, COEFFS, COEFFS)

    def far_step(group):
        picked = parent_table[group // LEVELS][far_rows[group]].reshape(PARENT_DEV, FAR_PARTNERS, SYSTEMS, COEFFS)
        return narrow(jnp.einsum('qfrk,qfkj->qrj', picked, far_blocks[group].astype(jnp.float32)))
    translated = lax.map(far_step, group_ids)
    spread = jnp.repeat(translated, CHILDREN, axis=1)
    returned = spread.reshape(GROUPS, GROUPS, PER_PEER, SYSTEMS, COEFFS).transpose(1, 0, 2, 3, 4)
    returned = returned.reshape(GROUPS, CLUSTER_DEV, SYSTEMS, COEFFS)

    def down_step(group):
        perm_row = order[group]
        expanded = narrow(jnp.einsum('srk,sjk->srj', returned[group], transfer_rows[group][perm_row].astype(jnp.float32)))
        slot_rows = jnp.einsum('srk,spk->rsp', expanded, basis_rows[group][perm_row].astype(jnp.float32))
        return jnp.zeros((SYSTEMS, CLUSTER_DEV, POINTS), jnp.float32).at[:, perm_row].set(slot_rows)
    far_sum = lax.map(down_step, group_ids).transpose(1, 0, 2, 3)
    return 0.5 * vector_in + (near_sum + far_sum).reshape(SYSTEMS, PANELS)

def reference(right_side, basis, transfer, order, far_src, far_mats, near_target, near_dest, near_src, near_blocks):

    def apply_op(vector_in):
        return operator(vector_in, basis, transfer, order, far_src, far_mats, near_target, near_dest, near_src, near_blocks)
    start_norm = jnp.sqrt(lax.optimization_barrier(jnp.sum(right_side * right_side, axis=1)) + EPSILON)
    basis_one = right_side / start_norm[:, None]
    image_one = apply_op(basis_one)
    along_one = lax.optimization_barrier(jnp.sum(basis_one * image_one, axis=1))
    remain = image_one - along_one[:, None] * basis_one
    rest_one = jnp.sqrt(lax.optimization_barrier(jnp.sum(remain * remain, axis=1)) + EPSILON)
    basis_two = remain / rest_one[:, None]
    image_two = apply_op(basis_two)
    cross_two = lax.optimization_barrier(jnp.sum(basis_one * image_two, axis=1))
    along_two = lax.optimization_barrier(jnp.sum(basis_two * image_two, axis=1))
    leftover = image_two - cross_two[:, None] * basis_one - along_two[:, None] * basis_two
    tail_sq = lax.optimization_barrier(jnp.sum(leftover * leftover, axis=1))
    gram_first = along_one * along_one + rest_one * rest_one
    gram_cross = along_one * cross_two + rest_one * along_two
    gram_last = cross_two * cross_two + along_two * along_two + tail_sq
    determinant = gram_first * gram_last - gram_cross * gram_cross
    coef_one = start_norm * (along_one * gram_last - cross_two * gram_cross) / determinant
    coef_two = start_norm * (gram_first * cross_two - gram_cross * along_one) / determinant
    solution = coef_one[:, None] * basis_one + coef_two[:, None] * basis_two
    residual = right_side - coef_one[:, None] * image_one - coef_two[:, None] * image_two
    return (solution, residual)
```

```python
import jax
import jax.numpy as jnp
from jax import lax
from jax.sharding import PartitionSpec as P

CHILDREN = 4


EPSILON = 1e-06
SCALE = 2.0**-20


def local(
    right_side,
    basis,
    transfer,
    order,
    far_src,
    far_mats,
    near_target,
    near_dest,
    near_src,
    near_blocks,
):
    systems = right_side.shape[0]
    clusters, points, coeffs = basis.shape
    groups = lax.axis_size(("leaf", "level"))
    capacity = max(4, 2 * near_dest.shape[0] // groups)
    parents = clusters // CHILDREN
    partners = far_src.shape[1]
    permutation = order[0]
    positions = jnp.arange(clusters, dtype=jnp.int32)
    inverse = jnp.zeros((clusters,), jnp.int32).at[permutation].set(positions)
    basis_slot = jnp.take(basis, permutation, axis=0)
    transfer_slot = jnp.take(transfer, permutation, axis=0)
    targets = near_dest[:, 0]
    member = (targets[:, None] == jnp.arange(groups, dtype=jnp.int32)[None, :]).astype(jnp.int32)
    slot_rank = jnp.sum(jnp.cumsum(member, axis=0) * member, axis=1) - 1
    slot_index = targets * capacity + slot_rank
    source_label = (
        jnp.full((groups * capacity,), -1.0, jnp.float32)
        .at[slot_index]
        .set(near_src.astype(jnp.float32))
    )
    cluster_ids = positions.astype(jnp.float32)

    def near_field(rounded):
        columns = jnp.take(rounded, near_target, axis=1)
        partial_rows = jnp.einsum(
            "rnp,npq->nrq", columns, near_blocks, preferred_element_type=jnp.float32
        )
        outgoing = (
            jnp.zeros((groups * capacity, systems, points), jnp.float32)
            .at[slot_index]
            .set(partial_rows)
        )
        incoming, labels = (
            lax.all_to_all(
                outgoing.astype(jnp.bfloat16),
                ("leaf", "level"),
                split_axis=0,
                concat_axis=0,
                tiled=True,
            ).astype(outgoing.dtype),
            lax.all_to_all(
                source_label.astype(jnp.bfloat16),
                ("leaf", "level"),
                split_axis=0,
                concat_axis=0,
                tiled=True,
            ).astype(source_label.dtype),
        )
        landing = (labels[:, None] == cluster_ids[None, :]).astype(jnp.float32)
        return jnp.einsum("sc,srp->rcp", landing, incoming, precision=lax.Precision.HIGHEST)

    def upward(lifted):
        arrived = lax.all_to_all(lifted, ("leaf", "level"), split_axis=0, concat_axis=0, tiled=True)
        return arrived

    def downward(spread):
        returned = lax.all_to_all(
            spread, ("leaf", "level"), split_axis=0, concat_axis=0, tiled=True
        )
        return returned

    def operator(vector_in):
        rounded = vector_in.astype(jnp.bfloat16).reshape(systems, clusters, points)
        near_sum = near_field(rounded)
        ordered = jnp.take(rounded, permutation, axis=1)
        expansion = jnp.einsum(
            "rsp,spk->srk", ordered, basis_slot, preferred_element_type=jnp.float32
        ).astype(jnp.bfloat16)
        lifted = jnp.einsum(
            "srk,skj->srj", expansion, transfer_slot, preferred_element_type=jnp.float32
        )
        arrived = upward(lifted)
        parent_rows = jnp.sum(arrived.reshape(parents, CHILDREN, systems, coeffs), axis=1).astype(
            jnp.bfloat16
        )
        parent_table = lax.all_gather(parent_rows, "level", axis=0, tiled=True)
        picked = jnp.take(parent_table, far_src.reshape(-1), axis=0).reshape(
            parents, partners, systems, coeffs
        )
        translated = jnp.einsum(
            "qfrk,qfkj->qrj", picked, far_mats, preferred_element_type=jnp.float32
        ).astype(jnp.bfloat16)
        returned = downward(jnp.repeat(translated, CHILDREN, axis=0))
        expanded = jnp.einsum(
            "srk,sjk->srj", returned, transfer_slot, preferred_element_type=jnp.float32
        ).astype(jnp.bfloat16)
        far_slot = jnp.einsum(
            "srk,spk->rsp", expanded, basis_slot, preferred_element_type=jnp.float32
        )
        far_sum = jnp.take(far_slot, inverse, axis=1)
        return near_sum + far_sum

    tiles = right_side.reshape(systems, clusters, points)
    image = operator(tiles)
    scaled = image * SCALE
    second = operator(scaled)
    own = jnp.stack(
        [
            jnp.sum(left * right, axis=(1, 2))
            for left, right in (
                (tiles, tiles),
                (tiles, image),
                (image, image),
                (tiles, second),
                (scaled, second),
                (second, second),
            )
        ]
    )
    dots = jnp.sum(lax.all_gather(own, ("leaf", "level")), axis=0)
    first_x, first_z, second_x, second_z, second_u = combine(dots)
    solved = first_x[:, None, None] * tiles + first_z[:, None, None] * image
    left_over = (
        second_x[:, None, None] * tiles
        + second_z[:, None, None] * image
        + second_u[:, None, None] * second
    )
    return solved.reshape(systems, -1), left_over.reshape(systems, -1)


def combine(dots):
    start_sq = dots[0] + EPSILON
    start_norm = jnp.sqrt(start_sq)
    xx, xz, zz, xu, zu, uu = (dots[k] / start_sq for k in range(6))
    along_one = 0.5 * xx + xz
    kappa = along_one - 0.5
    rest_raw = zz - 2.0 * kappa * xz + kappa * kappa * xx
    rest_sq = rest_raw + EPSILON
    rest_one = jnp.sqrt(rest_sq)
    scaled_rest = SCALE * rest_one
    scaled_sq = scaled_rest * scaled_rest
    xzs = SCALE * xz
    zzs = SCALE * SCALE * zz
    beta = (xz - kappa * xx) / rest_one
    gamma = rest_raw / rest_sq
    one_t = (xu - kappa * xzs) / scaled_rest
    two_t = (zu - kappa * zzs - SCALE * kappa * (xu - kappa * xzs)) / scaled_sq
    t_t = (uu - 2.0 * kappa * zu + kappa * kappa * zzs) / scaled_sq
    cross_two = 0.5 * beta + one_t
    along_two = 0.5 * gamma + two_t
    short = 0.5 - along_two
    tail_sq = (
        t_t
        + short * short * gamma
        + cross_two * cross_two * xx
        + 2.0 * short * two_t
        - 2.0 * cross_two * one_t
        - 2.0 * cross_two * short * beta
    )
    gram_first = along_one * along_one + rest_one * rest_one
    gram_cross = along_one * cross_two + rest_one * along_two
    gram_last = cross_two * cross_two + along_two * along_two + tail_sq
    determinant = gram_first * gram_last - gram_cross * gram_cross
    coef_one = start_norm * (along_one * gram_last - cross_two * gram_cross) / determinant
    coef_two = start_norm * (gram_first * cross_two - gram_cross * along_one) / determinant
    one = coef_one / start_norm
    two = coef_two / (start_norm * rest_one)
    return (
        one - kappa * two,
        two,
        1.0 - 0.5 * one + 0.5 * kappa * two,
        -one - (0.5 - kappa) * two,
        -coef_two / (start_norm * scaled_rest),
    )


def solution(mesh):
    placed = (
        P(None, ("leaf", "level")),
        P(("leaf", "level"), None, None),
        P(("leaf", "level"), None, None),
        P(("leaf", "level"), None),
        P(("leaf", "level"), None),
        P(("leaf", "level"), None, None, None),
        P(("leaf", "level")),
        P(("leaf", "level"), None),
        P(("leaf", "level")),
        P(("leaf", "level"), None, None),
    )
    return jax.shard_map(
        local,
        mesh=mesh,
        in_specs=placed,
        out_specs=(P(None, ("leaf", "level")), P(None, ("leaf", "level"))),
        check_vma=False,
    )
```

```python
import functools

import jax
import jax.numpy as jnp
from jax import lax
from jax.experimental import pallas as pl
from jax.experimental.pallas import tpu as pltpu
from jax.sharding import PartitionSpec as P

CHILDREN = 4
CAPACITY = 4
EPSILON = 1e-06
SCALE = 2.0**-20
AXES = ("leaf", "level")
LOGICAL = pl.DeviceIdType.LOGICAL
F32 = jnp.float32
BF16 = jnp.bfloat16


def combine(dots):
    start_sq = dots[0] + EPSILON
    start_norm = jnp.sqrt(start_sq)
    xx, xzs, zzs, xu, zu, uu = (dots[k] / start_sq for k in range(6))
    xz = xzs / SCALE
    zz = zzs / (SCALE * SCALE)
    along_one = 0.5 * xx + xz
    kappa = along_one - 0.5
    rest_raw = zz - 2.0 * kappa * xz + kappa * kappa * xx
    rest_sq = rest_raw + EPSILON
    rest_one = jnp.sqrt(rest_sq)
    scaled_rest = SCALE * rest_one
    scaled_sq = scaled_rest * scaled_rest
    beta = (xz - kappa * xx) / rest_one
    gamma = rest_raw / rest_sq
    one_t = (xu - kappa * xzs) / scaled_rest
    two_t = (zu - kappa * zzs - SCALE * kappa * (xu - kappa * xzs)) / scaled_sq
    t_t = (uu - 2.0 * kappa * zu + kappa * kappa * zzs) / scaled_sq
    cross_two = 0.5 * beta + one_t
    along_two = 0.5 * gamma + two_t
    short = 0.5 - along_two
    tail_sq = (
        t_t
        + short * short * gamma
        + cross_two * cross_two * xx
        + 2.0 * short * two_t
        - 2.0 * cross_two * one_t
        - 2.0 * cross_two * short * beta
    )
    gram_first = along_one * along_one + rest_one * rest_one
    gram_cross = along_one * cross_two + rest_one * along_two
    gram_last = cross_two * cross_two + along_two * along_two + tail_sq
    determinant = gram_first * gram_last - gram_cross * gram_cross
    coef_one = start_norm * (along_one * gram_last - cross_two * gram_cross) / determinant
    coef_two = start_norm * (gram_first * cross_two - gram_cross * along_one) / determinant
    one = coef_one / start_norm
    two = coef_two / (start_norm * rest_one)
    scaled_two = coef_two / (start_norm * scaled_rest)
    return (
        one - kappa * two,
        scaled_two,
        1.0 - 0.5 * one + 0.5 * kappa * two,
        -one / SCALE - (0.5 - kappa) * scaled_two,
        -scaled_two,
    )


def loop(count, unroll, body):
    def step(block, carry):
        for u in range(unroll):
            body(block * unroll + u)
        return carry

    lax.fori_loop(0, count // unroll, step, 0)


def kernel(
    target_ref, order_ref, far_ref, inverse_ref, source_ref, perm_ref, keep_ref, last_ref,
    x_hbm, basis_hbm, transfer_hbm, far_hbm, near_hbm,
    solved_ref, left_ref,
    x_ref, z_ref, u_ref, basis_ref, transfer_ref, product_ref, far_w, near_w,
    part_ref, lifted_ref, field_ref, run_ref,
    up_send, up_recv, down_send, near_send,
    table_one, table_two, down_one, down_two, near_one, near_two, cast_one, cast_two,
    dot_send, dot_recv,
    load_sem, remote_sem,
):
    clusters = basis_ref.shape[0]
    devices = clusters
    levels = lax.axis_size("level")
    leaf, level = lax.axis_index("leaf"), lax.axis_index("level")
    me = leaf * levels + level
    pairs = near_w.shape[0]
    parents = clusters // CHILDREN
    partners = far_w.shape[0] // parents
    lanes = basis_ref.shape[1]
    chunks = 8
    rows = clusters // chunks

    loads = [pltpu.make_async_copy(x_hbm, x_ref, load_sem.at[0])]
    for k in range(chunks):
        part = pl.ds(k * rows, rows)
        loads.append(
            pltpu.make_async_copy(basis_hbm.at[part], basis_ref.at[part], load_sem.at[1 + 2 * k])
        )
        loads.append(
            pltpu.make_async_copy(
                transfer_hbm.at[part], transfer_ref.at[part], load_sem.at[2 + 2 * k]
            )
        )
    load_near = pltpu.make_async_copy(near_hbm, near_w, load_sem.at[1 + 2 * chunks])
    load_far = pltpu.make_async_copy(far_hbm, far_w, load_sem.at[2 + 2 * chunks])
    for copy in loads:
        copy.start()
    load_near.start()
    load_far.start()

    barrier = pltpu.get_barrier_semaphore()

    def greet(i, carry):
        pl.semaphore_signal(
            barrier, inc=1, device_id=(me + i) % devices, device_id_type=LOGICAL
        )
        return carry

    lax.fori_loop(1, devices, greet, 0, unroll=8)

    def push(src, dst, stage, device):
        pltpu.make_async_remote_copy(
            src_ref=src,
            dst_ref=dst,
            send_sem=remote_sem.at[stage, 0],
            recv_sem=remote_sem.at[stage, 1],
            device_id=device,
            device_id_type=LOGICAL,
        ).start()

    def settle(ref, stage):
        for end in range(2):
            pltpu.make_async_copy(ref, ref, remote_sem.at[stage, end]).wait()

    def push_all(lo, hi, stage, src, dst):
        def go(i, carry):
            other = (me + i) % devices
            push(src(other), dst, stage, other)
            return carry

        lax.fori_loop(lo, hi, go, 0, unroll=8)

    def tile(ref, c):
        return ref[:, pl.ds(pl.multiple_of(c * lanes, lanes), lanes)]

    run_ref[CAPACITY * devices] = jnp.zeros(run_ref.shape[1:], F32)

    for trip, (v_ref, o_ref, scale) in enumerate(((x_ref, z_ref, SCALE), (z_ref, u_ref, 1.0))):
        first = trip == 0
        stage = 4 * trip
        table_ref = table_one if first else table_two
        down_recv = down_one if first else down_two
        near_recv = near_one if first else near_two
        cast_ref = cast_one if first else cast_two

        def lift(c):
            value = tile(v_ref, c).astype(BF16)
            cast_ref[c] = value
            lifted_ref[c] = jnp.dot(value, product_ref[c], preferred_element_type=F32)

        if first:
            loads[0].wait()

            for k in range(chunks):
                loads[1 + 2 * k].wait()
                loads[2 + 2 * k].wait()

                def fuse(c, k=k):
                    product_ref[k * rows + c] = jnp.dot(
                        basis_ref[k * rows + c],
                        transfer_ref[k * rows + c],
                        preferred_element_type=F32,
                    ).astype(BF16)

                loop(rows, 8, fuse)
        loop(clusters, 16, lift)

        def order_up(s):
            up_send[trip, s] = lifted_ref[order_ref[s]].astype(BF16)

        loop(clusters, 16, order_up)
        up_recv[trip, me] = lifted_ref[order_ref[me]].astype(BF16)
        if first:
            pl.semaphore_wait(barrier, devices - 1)
        push_all(1, devices, stage, lambda e: up_send.at[trip, e], up_recv.at[trip, me])

        if first:
            load_near.wait()

        def near_product(n):
            part_ref[n] = jnp.dot(
                cast_ref[target_ref[n]], near_w[n], preferred_element_type=F32
            )

        loop(pairs, 32, near_product)

        def place(s):
            near_send[trip, s] = part_ref[source_ref[s]].astype(BF16)

        loop(CAPACITY * devices, 16, place)
        for k in range(CAPACITY):
            near_recv[CAPACITY * me + k] = part_ref[
                source_ref[CAPACITY * me + k]
            ].astype(BF16)

        def near_push(lo, hi):
            push_all(
                lo,
                hi,
                stage + 3,
                lambda e: near_send.at[trip, pl.ds(CAPACITY * e, CAPACITY)],
                near_recv.at[pl.ds(CAPACITY * me, CAPACITY)],
            )

        near_push(1, 43)
        settle(up_recv.at[trip, pl.ds(0, devices - 1)], stage)

        def gather_parent(q):
            total = up_recv[trip, CHILDREN * q].astype(F32)
            for i in range(1, CHILDREN):
                total = total + up_recv[trip, CHILDREN * q + i].astype(F32)
            table_ref[level * parents + q] = total.astype(BF16)

        loop(parents, 8, gather_parent)
        mine = table_ref.at[pl.ds(level * parents, parents)]
        for i in range(1, CHILDREN):
            push(mine, mine, stage + 1, leaf * levels + (level + i) % levels)
        near_push(43, 85)
        if first:
            load_far.wait()
        settle(table_ref.at[pl.ds(0, (levels - 1) * parents)], stage + 1)

        def translate(q):
            picked = jnp.concatenate(
                [table_ref[far_ref[partners * q + k]] for k in range(partners)], axis=1
            )
            mats = far_w[pl.ds(partners * q, partners)].reshape(partners * lanes, lanes)
            down_send[trip, q] = jnp.dot(picked, mats, preferred_element_type=F32).astype(BF16)

        loop(parents, 8, translate)
        down_recv[me] = down_send[trip, me // CHILDREN]
        push_all(
            1, devices, stage + 2, lambda e: down_send.at[trip, e // CHILDREN], down_recv.at[me]
        )
        near_push(85, devices)
        settle(down_recv.at[pl.ds(0, devices - 1)], stage + 2)

        def spread(c):
            field_ref[c] = lax.dot_general(
                down_recv[inverse_ref[c]],
                product_ref[c],
                (((1,), (1,)), ((), ())),
                preferred_element_type=F32,
            )

        loop(clusters, 16, spread)
        settle(near_recv.at[pl.ds(0, CAPACITY * (devices - 1))], stage + 3)

        def land(block, total):
            for u in range(8):
                i = block * 8 + u
                total = total * keep_ref[i].astype(F32) + near_recv[perm_ref[i]].astype(F32)
                run_ref[i] = total
            return total

        lax.fori_loop(0, CAPACITY * devices // 8, land, jnp.zeros(run_ref.shape[1:], F32))

        def finish(c):
            value = field_ref[c] + run_ref[last_ref[c]]
            if scale != 1.0:
                value = value * scale
            o_ref[:, pl.ds(pl.multiple_of(c * lanes, lanes), lanes)] = value

        loop(clusters, 16, finish)

    systems = x_ref.shape[0]

    def products(block, sums):
        sums = list(sums)
        for u in range(4):
            x, z, w = (tile(ref, block * 4 + u) for ref in (x_ref, z_ref, u_ref))
            for k, (a, b) in enumerate(((x, x), (x, z), (z, z), (x, w), (z, w), (w, w))):
                sums[k] = sums[k] + a * b
        return tuple(sums)

    zero = jnp.zeros((systems, lanes), F32)
    sums = lax.fori_loop(0, clusters // 4, products, (zero,) * 6)
    lane = lax.broadcasted_iota(jnp.int32, (systems, lanes), 1)
    row = lax.broadcasted_iota(jnp.int32, (systems, lanes), 0)
    packed = zero
    for k, total in enumerate(sums):
        packed = jnp.where(
            lane == row + k * systems, jnp.sum(total, axis=1, keepdims=True), packed
        )
    packed = jnp.sum(packed, axis=0, keepdims=True)
    dot_send[...] = packed
    dot_recv[pl.ds(me, 1)] = packed[None]
    push_all(1, devices, 8, lambda e: dot_send, dot_recv.at[me])
    for end, ref in ((0, dot_recv), (1, dot_recv)):
        ref = ref.at[pl.ds(0, devices - 1)]
        pltpu.make_async_copy(ref, ref, remote_sem.at[8, end]).wait()
    gathered = jnp.sum(dot_recv[...], axis=0)
    spread_out = jnp.broadcast_to(gathered, (systems, lanes))
    dots = [
        jnp.sum(jnp.where(lane == row + k * systems, spread_out, 0.0), axis=1, keepdims=True)
        for k in range(6)
    ]
    first_x, first_z, second_x, second_z, second_u = (
        jnp.broadcast_to(value, (systems, lanes)) for value in combine(dots)
    )

    def write(c):
        where = pl.ds(pl.multiple_of(c * lanes, lanes), lanes)
        x, z, w = x_ref[:, where], z_ref[:, where], u_ref[:, where]
        solved_ref[:, where] = first_x * x + first_z * z
        left_ref[:, where] = second_x * x + second_z * z + second_u * w

    loop(clusters, 8, write)


def local(
    right_side,
    basis,
    transfer,
    order,
    far_src,
    far_mats,
    near_target,
    near_dest,
    near_src,
    near_blocks,
):
    systems, panels = right_side.shape
    clusters, points, coeffs = basis.shape
    devices = lax.axis_size(AXES)
    pairs = near_target.shape[0]
    parents = clusters // CHILDREN
    slots = CAPACITY * devices

    def ints(values):
        return values.astype(jnp.int32)

    index = jnp.arange(clusters, dtype=jnp.int32)
    inverse = jnp.sum(ints(order[0][None, :] == index[:, None]) * index[None, :], axis=1)
    dest = near_dest[:, 0]
    number = jnp.arange(pairs, dtype=jnp.int32)
    rank = jnp.sum(ints((dest[None, :] == dest[:, None]) & (number[None, :] < number[:, None])), axis=1)
    slot = dest * CAPACITY + rank
    every = jnp.arange(slots, dtype=jnp.int32)
    here = ints(slot[None, :] == every[:, None])
    source = jnp.sum(here * number[None, :], axis=1)
    label = jnp.sum(here * (near_src[None, :] - clusters), axis=1) + clusters
    labels = lax.all_to_all(
        label.reshape(devices, CAPACITY), AXES, split_axis=0, concat_axis=0, tiled=True
    ).reshape(slots)
    less = ints(labels[None, :] < labels[:, None])
    tied = ints((labels[None, :] == labels[:, None]) & (every[None, :] < every[:, None]))
    below = jnp.sum(less, axis=1)
    position = below + jnp.sum(tied, axis=1)
    there = ints(position[None, :] == every[:, None])
    perm = jnp.sum(there * every[None, :], axis=1)
    keep = ints(jnp.sum(there * below[None, :], axis=1) != every)
    upto = jnp.sum(ints(labels[None, :] <= index[:, None]), axis=1)
    some = jnp.sum(ints(labels[None, :] == index[:, None]), axis=1)
    last = jnp.where(some > 0, upto - 1, slots)

    smem = pl.BlockSpec(memory_space=pltpu.SMEM)
    hbm = pl.BlockSpec(memory_space=pl.ANY)
    vmem = pl.BlockSpec(memory_space=pltpu.VMEM)
    field = jax.ShapeDtypeStruct((systems, panels), F32)
    cell = (systems, points)
    return pl.pallas_call(
        kernel,
        name="gmres",
        out_shape=(field, field),
        in_specs=[smem] * 8 + [hbm] * 5,
        out_specs=(vmem, vmem),
        scratch_shapes=[
            pltpu.VMEM((systems, panels), F32),
            pltpu.VMEM((systems, panels), F32),
            pltpu.VMEM((systems, panels), F32),
            pltpu.VMEM(basis.shape, BF16),
            pltpu.VMEM(transfer.shape, BF16),
            pltpu.VMEM(basis.shape, BF16),
            pltpu.VMEM((parents * far_src.shape[1], coeffs, coeffs), BF16),
            pltpu.VMEM(near_blocks.shape, BF16),
            pltpu.VMEM((pairs, *cell), F32),
            pltpu.VMEM((clusters, *cell), F32),
            pltpu.VMEM((clusters, *cell), F32),
            pltpu.VMEM((slots + 8, *cell), F32),
            pltpu.VMEM((2, clusters, *cell), BF16),
            pltpu.VMEM((2, clusters, *cell), BF16),
            pltpu.VMEM((2, parents, *cell), BF16),
            pltpu.VMEM((2, slots, *cell), BF16),
            pltpu.VMEM((CHILDREN * parents, *cell), BF16),
            pltpu.VMEM((CHILDREN * parents, *cell), BF16),
            pltpu.VMEM((clusters, *cell), BF16),
            pltpu.VMEM((clusters, *cell), BF16),
            pltpu.VMEM((slots, *cell), BF16),
            pltpu.VMEM((slots, *cell), BF16),
            pltpu.VMEM((clusters, *cell), BF16),
            pltpu.VMEM((clusters, *cell), BF16),
            pltpu.VMEM((1, points), F32),
            pltpu.VMEM((devices, 1, points), F32),
            pltpu.SemaphoreType.DMA((19,)),
            pltpu.SemaphoreType.DMA((9, 2)),
        ],
        compiler_params=pltpu.CompilerParams(
            collective_id=0, has_side_effects=True, vmem_limit_bytes=60 << 20
        ),
    )(
        near_target,
        order.reshape(-1),
        far_src.reshape(-1),
        inverse,
        source,
        perm,
        keep,
        last,
        right_side,
        basis,
        transfer,
        far_mats.reshape(-1, coeffs, coeffs),
        near_blocks,
    )


def solution(mesh):
    placed = (
        P(None, AXES),
        P(AXES, None, None),
        P(AXES, None, None),
        P(AXES, None),
        P(AXES, None),
        P(AXES, None, None, None),
        P(AXES),
        P(AXES, None),
        P(AXES),
        P(AXES, None, None),
    )
    return jax.shard_map(
        local,
        mesh=mesh,
        in_specs=placed,
        out_specs=(P(None, AXES), P(None, AXES)),
        check_vma=False,
    )
```

```python
import functools

import jax
import jax.numpy as jnp
from jax import lax
from jax.experimental import pallas as pl
from jax.experimental.pallas import tpu as pltpu
from jax.sharding import PartitionSpec as P

CHILDREN = 4
CAPACITY = 4
EPSILON = 1e-06
SCALE = 2.0**-20
STRIDE = 37
AXES = ("leaf", "level")
LOGICAL = pl.DeviceIdType.LOGICAL
F32 = jnp.float32
BF16 = jnp.bfloat16


def combine(dots):
    start_sq = dots[0] + EPSILON
    start_norm = jnp.sqrt(start_sq)
    xx, xzs, zzs, xu, zu, uu = (dots[k] / start_sq for k in range(6))
    xz = xzs / SCALE
    zz = zzs / (SCALE * SCALE)
    along_one = 0.5 * xx + xz
    kappa = along_one - 0.5
    rest_raw = zz - 2.0 * kappa * xz + kappa * kappa * xx
    rest_sq = rest_raw + EPSILON
    rest_one = jnp.sqrt(rest_sq)
    scaled_rest = SCALE * rest_one
    scaled_sq = scaled_rest * scaled_rest
    beta = (xz - kappa * xx) / rest_one
    gamma = rest_raw / rest_sq
    one_t = (xu - kappa * xzs) / scaled_rest
    two_t = (zu - kappa * zzs - SCALE * kappa * (xu - kappa * xzs)) / scaled_sq
    t_t = (uu - 2.0 * kappa * zu + kappa * kappa * zzs) / scaled_sq
    cross_two = 0.5 * beta + one_t
    along_two = 0.5 * gamma + two_t
    short = 0.5 - along_two
    tail_sq = (
        t_t
        + short * short * gamma
        + cross_two * cross_two * xx
        + 2.0 * short * two_t
        - 2.0 * cross_two * one_t
        - 2.0 * cross_two * short * beta
    )
    gram_first = along_one * along_one + rest_one * rest_one
    gram_cross = along_one * cross_two + rest_one * along_two
    gram_last = cross_two * cross_two + along_two * along_two + tail_sq
    determinant = gram_first * gram_last - gram_cross * gram_cross
    coef_one = start_norm * (along_one * gram_last - cross_two * gram_cross) / determinant
    coef_two = start_norm * (gram_first * cross_two - gram_cross * along_one) / determinant
    one = coef_one / start_norm
    two = coef_two / (start_norm * rest_one)
    scaled_two = coef_two / (start_norm * scaled_rest)
    return (
        one - kappa * two,
        scaled_two,
        1.0 - 0.5 * one + 0.5 * kappa * two,
        -one / SCALE - (0.5 - kappa) * scaled_two,
        -scaled_two,
    )


def loop(count, unroll, body):
    def step(block, carry):
        for u in range(unroll):
            body(block * unroll + u)
        return carry

    lax.fori_loop(0, count // unroll, step, 0)


def send_tables(dest, source, order, slots, labels):
    size = order.shape[1]
    lane = lax.broadcasted_iota(jnp.int32, (size, size), 1)
    row = lax.broadcasted_iota(jnp.int32, (size, size), 0)

    def upright(values):
        return jnp.sum(jnp.where(lane == row, values, 0), axis=1, keepdims=True)

    halves = dest.shape[0]
    dest_row = [dest[h : h + 1, :] for h in range(halves)]
    dest_col = [upright(values) for values in dest_row]
    source_col = [upright(source[h : h + 1, :]) for h in range(halves)]
    rank = []
    for h in range(halves):
        total = jnp.zeros((size, 1), jnp.int32)
        for g in range(h + 1):
            same = dest_col[h] == dest_row[g]
            if g == h:
                same = same & (lane < row)
            total = total + jnp.sum(jnp.where(same, 1, 0), axis=1, keepdims=True)
        rank.append(total)
    every = []
    for k in range(CAPACITY):
        pair = jnp.zeros((1, size), jnp.int32)
        label = jnp.full((1, size), size, jnp.int32)
        for h in range(halves):
            chosen = (dest_col[h] == lane) & (rank[h] == k)
            pair = pair + jnp.sum(jnp.where(chosen, row + h * size, 0), axis=0, keepdims=True)
            label = label + jnp.sum(
                jnp.where(chosen, source_col[h] - size, 0), axis=0, keepdims=True
            )
        slots[pl.ds(k, 1), :] = pair
        every.append(label)
    inverse = jnp.sum(jnp.where(upright(order) == lane, row, 0), axis=0, keepdims=True)
    slots[pl.ds(CAPACITY, 1), :] = jnp.minimum(inverse, size - 1)
    mixed = jnp.zeros((size, size), jnp.int32)
    for k in range(CAPACITY):
        mixed = jnp.where(lane == k, upright(every[k]), mixed)
    labels[...] = mixed.astype(F32).reshape(labels.shape)


def land_tables(labels, out):
    size = labels.shape[0]
    lane = lax.broadcasted_iota(jnp.int32, (size, size), 1)
    row = lax.broadcasted_iota(jnp.int32, (size, size), 0)
    columns = [labels[:, k : k + 1] for k in range(CAPACITY)]
    rows = [
        jnp.sum(jnp.where(lane == row, columns[k], 0), axis=0, keepdims=True)
        for k in range(CAPACITY)
    ]
    upto = jnp.zeros((size, size), jnp.int32)
    some = jnp.zeros((size, size), jnp.int32)
    perm = [jnp.zeros((size, size), jnp.int32) for _ in range(CAPACITY)]
    first = [jnp.zeros((size, size), jnp.int32) for _ in range(CAPACITY)]
    for k in range(CAPACITY):
        less = jnp.zeros((size, size), jnp.int32)
        tied = jnp.zeros((size, size), jnp.int32)
        for j in range(CAPACITY):
            less = less + jnp.where(rows[j] < columns[k], 1, 0)
            if j < k:
                tied = tied + jnp.where(rows[j] == columns[k], 1, 0)
            elif j == k:
                tied = tied + jnp.where((rows[j] == columns[k]) & (lane < row), 1, 0)
        below = jnp.sum(less, axis=1, keepdims=True)
        place = below + jnp.sum(tied, axis=1, keepdims=True)
        upto = upto + jnp.where(columns[k] <= lane, 1, 0)
        some = some + jnp.where(columns[k] == lane, 1, 0)
        for b in range(CAPACITY):
            here = place == lane + b * size
            perm[b] = perm[b] + jnp.where(here, CAPACITY * row + k, 0)
            first[b] = first[b] + jnp.where(here, below, 0)
    for b in range(CAPACITY):
        out[pl.ds(b, 1), :] = jnp.sum(perm[b], axis=0, keepdims=True)
        start = jnp.sum(first[b], axis=0, keepdims=True)
        out[pl.ds(CAPACITY + b, 1), :] = jnp.where(start == lane[0:1] + b * size, 0, 1)
    ends = jnp.sum(upto, axis=0, keepdims=True) - 1
    out[pl.ds(2 * CAPACITY, 1), :] = jnp.where(
        jnp.sum(some, axis=0, keepdims=True) > 0, ends, CAPACITY * size
    )


def kernel(
    target_ref, order_ref, far_ref,
    dest_ref, source_ref, order_row,
    x_hbm, basis_hbm, transfer_hbm, far_hbm, near_hbm,
    z_ref, u_ref, coef_ref,
    x_ref, basis_ref, transfer_ref, product_ref, turned_ref, far_w, near_w,
    part_ref, field_ref, run_ref,
    up_send, up_recv, down_send, near_send,
    table_one, table_two, down_one, down_two, near_one, near_two, cast_one, cast_two,
    dot_send, dot_recv, label_send, label_recv,
    slot_rows, land_rows, slot_of, land_of,
    load_sem, table_sem, remote_sem,
):
    clusters = basis_ref.shape[0]
    devices = clusters
    levels = lax.axis_size("level")
    leaf, level = lax.axis_index("leaf"), lax.axis_index("level")
    leaves = devices // levels
    me = leaf * levels + level
    pairs = near_w.shape[0]
    parents = clusters // CHILDREN
    partners = far_w.shape[0] // parents
    lanes = basis_ref.shape[1]
    systems = x_ref.shape[0]
    chunks = 8
    rows = clusters // chunks

    load_x = pltpu.make_async_copy(x_hbm, x_ref, load_sem.at[0])
    loads = []
    for k in range(chunks):
        part = pl.ds(k * rows, rows)
        loads.append(
            pltpu.make_async_copy(basis_hbm.at[part], basis_ref.at[part], load_sem.at[1 + 2 * k])
        )
        loads.append(
            pltpu.make_async_copy(
                transfer_hbm.at[part], transfer_ref.at[part], load_sem.at[2 + 2 * k]
            )
        )
    load_near = pltpu.make_async_copy(near_hbm, near_w, load_sem.at[1 + 2 * chunks])
    load_far = pltpu.make_async_copy(far_hbm, far_w, load_sem.at[2 + 2 * chunks])
    load_x.start()
    for copy in loads:
        copy.start()
    load_near.start()
    load_far.start()

    def peer(i):
        return (me + STRIDE * i) % devices

    barrier = pltpu.get_barrier_semaphore()

    def greet(i, carry):
        pl.semaphore_signal(barrier, inc=1, device_id=peer(i), device_id_type=LOGICAL)
        return carry

    lax.fori_loop(1, devices, greet, 0, unroll=8)

    def push(src, dst, stage, device):
        pltpu.make_async_remote_copy(
            src_ref=src,
            dst_ref=dst,
            send_sem=remote_sem.at[stage, 0],
            recv_sem=remote_sem.at[stage, 1],
            device_id=device,
            device_id_type=LOGICAL,
        ).start()

    def settle(ref, stage):
        for end in range(2):
            pltpu.make_async_copy(ref, ref, remote_sem.at[stage, end]).wait()

    def push_all(lo, hi, stage, src, dst):
        def go(i, carry):
            other = peer(i)
            push(src(other), dst, stage, other)
            return carry

        lax.fori_loop(lo, hi, go, 0, unroll=8)

    def tile(ref, c):
        return ref[:, pl.ds(pl.multiple_of(c * lanes, lanes), lanes)]

    send_tables(dest_ref[...], source_ref[...], order_row[...], slot_rows, label_send)
    move_slots = pltpu.make_async_copy(slot_rows, slot_of, table_sem.at[0])
    move_slots.start()
    run_ref[CAPACITY * devices] = jnp.zeros(run_ref.shape[1:], F32)
    load_x.wait()

    def cast(c):
        cast_one[c] = tile(x_ref, c).astype(BF16)

    loop(clusters, 16, cast)
    for k in range(chunks):
        loads[2 * k].wait()
        loads[2 * k + 1].wait()

        def fuse(c, k=k):
            product_ref[k * rows + c] = jnp.dot(
                basis_ref[k * rows + c], transfer_ref[k * rows + c], preferred_element_type=F32
            ).astype(BF16)

        loop(rows, 8, fuse)
    move_slots.wait()
    pl.semaphore_wait(barrier, devices - 1)

    zero = jnp.zeros((systems, lanes), F32)
    dots = []
    for trip in range(2):
        first = trip == 0
        stage = 4 * trip
        table_ref = table_one if first else table_two
        down_recv = down_one if first else down_two
        near_recv = near_one if first else near_two
        cast_ref = cast_one if first else cast_two

        def lift(s):
            c = order_ref[s]
            return jnp.dot(cast_ref[c], product_ref[c], preferred_element_type=F32).astype(BF16)

        def up(i, carry):
            other = peer(i)
            up_send[trip, other] = lift(other)
            push(up_send.at[trip, other], up_recv.at[trip, me], stage, other)
            return carry

        lax.fori_loop(1, devices, up, 0, unroll=8)
        up_recv[trip, me] = lift(me)

        if first:
            load_near.wait()

        def near_product(n):
            part_ref[n] = jnp.dot(
                cast_ref[target_ref[n]], near_w[n], preferred_element_type=F32
            )

        loop(pairs, 32, near_product)

        def place(d):
            for k in range(CAPACITY):
                near_send[trip, CAPACITY * d + k] = part_ref[slot_of[k, d]].astype(BF16)

        loop(devices, 4, place)
        for k in range(CAPACITY):
            near_recv[CAPACITY * me + k] = part_ref[slot_of[k, me]].astype(BF16)

        def near_push(lo, hi):
            push_all(
                lo,
                hi,
                stage + 3,
                lambda e: near_send.at[trip, pl.ds(CAPACITY * e, CAPACITY)],
                near_recv.at[pl.ds(CAPACITY * me, CAPACITY)],
            )

        near_push(1, 43)
        if first:
            label_recv[pl.ds(me, 1)] = label_send[pl.ds(me, 1)]
            push_all(1, devices, 9, lambda e: label_send.at[e], label_recv.at[me])
        settle(up_recv.at[trip, pl.ds(0, devices - 1)], stage)

        def gather_parent(q):
            total = up_recv[trip, CHILDREN * q].astype(F32)
            for i in range(1, CHILDREN):
                total = total + up_recv[trip, CHILDREN * q + i].astype(F32)
            table_ref[level * parents + q] = total.astype(BF16)

        loop(parents, 8, gather_parent)
        mine = table_ref.at[pl.ds(level * parents, parents)]
        for i in range(1, CHILDREN):
            push(mine, mine, stage + 1, leaf * levels + (level + i) % levels)
        near_push(43, 85)
        if first:

            def turn(c):
                turned_ref[c] = product_ref[c].T

            loop(clusters, 8, turn)
            load_far.wait()
        settle(table_ref.at[pl.ds(0, (levels - 1) * parents)], stage + 1)

        def translate(q):
            picked = jnp.concatenate(
                [table_ref[far_ref[k, q]] for k in range(partners)], axis=1
            )
            mats = far_w[pl.ds(partners * q, partners)].reshape(partners * lanes, lanes)
            return jnp.dot(picked, mats, preferred_element_type=F32).astype(BF16)

        def down(q, skip):
            value = translate(q)
            down_send[trip, q] = value
            for i in range(skip, levels):
                push(
                    down_send.at[trip, q],
                    down_recv.at[me],
                    stage + 2,
                    q * levels + (level + i) % levels,
                )
            return value

        down_recv[me] = down(leaf, 1)

        def down_step(j, carry):
            down((leaf + 13 * j) % leaves, 0)
            return carry

        lax.fori_loop(1, leaves, down_step, 0, unroll=4)
        near_push(85, devices)
        if first:
            settle(label_recv.at[pl.ds(0, devices - 1)], 9)
            land_tables(
                label_recv[...].reshape(devices, lanes).astype(jnp.int32), land_rows
            )
            move_land = pltpu.make_async_copy(land_rows, land_of, table_sem.at[1])
            move_land.start()
            move_land.wait()
        settle(down_recv.at[pl.ds(0, devices - 1)], stage + 2)

        def spread(c):
            field_ref[c] = jnp.dot(
                down_recv[slot_of[CAPACITY, c]], turned_ref[c], preferred_element_type=F32
            )

        loop(clusters, 32, spread)
        settle(near_recv.at[pl.ds(0, CAPACITY * (devices - 1))], stage + 3)

        for b in range(CAPACITY):

            def land(block, total):
                for u in range(8):
                    i = block * 8 + u
                    total = total * land_of[CAPACITY + b, i].astype(F32) + near_recv[
                        land_of[b, i]
                    ].astype(F32)
                    run_ref[b * devices + i] = total
                return total

            total = lax.fori_loop(0, devices // 8, land, zero if b == 0 else total)

        def finish(block, sums):
            sums = list(sums)
            for u in range(8):
                c = block * 8 + u
                where = pl.ds(pl.multiple_of(c * lanes, lanes), lanes)
                value = field_ref[c] + run_ref[land_of[2 * CAPACITY, c]]
                x = x_ref[:, where]
                if first:
                    value = value * SCALE
                    z_ref[:, where] = value
                    cast_two[c] = value.astype(BF16)
                    terms = ((x, x), (x, value), (value, value))
                else:
                    u_ref[:, where] = value
                    terms = ((x, value), (z_ref[:, where], value), (value, value))
                for k, (p, q) in enumerate(terms):
                    sums[k] = sums[k] + p * q
            return tuple(sums)

        dots += lax.fori_loop(0, clusters // 8, finish, (zero,) * 3)

    lane = lax.broadcasted_iota(jnp.int32, (systems, lanes), 1)
    row = lax.broadcasted_iota(jnp.int32, (systems, lanes), 0)
    packed = zero
    for k, total in enumerate(dots):
        packed = jnp.where(
            lane == row + k * systems, jnp.sum(total, axis=1, keepdims=True), packed
        )
    packed = jnp.sum(packed, axis=0, keepdims=True)
    dot_send[...] = packed
    dot_recv[pl.ds(me, 1)] = packed[None]
    push_all(1, devices, 8, lambda e: dot_send, dot_recv.at[me])
    settle(dot_recv.at[pl.ds(0, devices - 1)], 8)
    gathered = jnp.broadcast_to(jnp.sum(dot_recv[...], axis=0), (systems, lanes))
    scalars = combine(
        [
            jnp.sum(jnp.where(lane == row + k * systems, gathered, 0.0), axis=1, keepdims=True)
            for k in range(len(dots))
        ]
    )
    for k, value in enumerate(scalars):
        coef_ref[k] = jnp.broadcast_to(value, (systems, lanes))


def local(
    right_side,
    basis,
    transfer,
    order,
    far_src,
    far_mats,
    near_target,
    near_dest,
    near_src,
    near_blocks,
):
    systems, panels = right_side.shape
    clusters, points, coeffs = basis.shape
    devices = lax.axis_size(AXES)
    pairs = near_target.shape[0]
    parents = clusters // CHILDREN
    slots = CAPACITY * devices
    smem = pl.BlockSpec(memory_space=pltpu.SMEM)
    hbm = pl.BlockSpec(memory_space=pl.ANY)
    vmem = pl.BlockSpec(memory_space=pltpu.VMEM)
    field = jax.ShapeDtypeStruct((systems, panels), F32)
    cell = (systems, points)
    image, second, coefs = pl.pallas_call(
        kernel,
        name="gmres",
        out_shape=(field, field, jax.ShapeDtypeStruct((5, systems, points), F32)),
        in_specs=[smem] * 3 + [vmem] * 3 + [hbm] * 5,
        out_specs=(vmem, vmem, vmem),
        scratch_shapes=[
            pltpu.VMEM((systems, panels), F32),
            pltpu.VMEM(basis.shape, BF16),
            pltpu.VMEM(transfer.shape, BF16),
            pltpu.VMEM(basis.shape, BF16),
            pltpu.VMEM(basis.shape, BF16),
            pltpu.VMEM((parents * far_src.shape[1], coeffs, coeffs), BF16),
            pltpu.VMEM(near_blocks.shape, BF16),
            pltpu.VMEM((pairs, *cell), F32),
            pltpu.VMEM((clusters, *cell), F32),
            pltpu.VMEM((slots + 8, *cell), F32),
            pltpu.VMEM((2, clusters, *cell), BF16),
            pltpu.VMEM((2, clusters, *cell), BF16),
            pltpu.VMEM((2, parents, *cell), BF16),
            pltpu.VMEM((2, slots, *cell), BF16),
            pltpu.VMEM((CHILDREN * parents, *cell), BF16),
            pltpu.VMEM((CHILDREN * parents, *cell), BF16),
            pltpu.VMEM((clusters, *cell), BF16),
            pltpu.VMEM((clusters, *cell), BF16),
            pltpu.VMEM((slots, *cell), BF16),
            pltpu.VMEM((slots, *cell), BF16),
            pltpu.VMEM((clusters, *cell), BF16),
            pltpu.VMEM((clusters, *cell), BF16),
            pltpu.VMEM((1, points), F32),
            pltpu.VMEM((devices, 1, points), F32),
            pltpu.VMEM((devices, 1, points), F32),
            pltpu.VMEM((devices, 1, points), F32),
            pltpu.VMEM((8, devices), jnp.int32),
            pltpu.VMEM((16, devices), jnp.int32),
            pltpu.SMEM((8, devices), jnp.int32),
            pltpu.SMEM((16, devices), jnp.int32),
            pltpu.SemaphoreType.DMA((19,)),
            pltpu.SemaphoreType.DMA((2,)),
            pltpu.SemaphoreType.DMA((10, 2)),
        ],
        compiler_params=pltpu.CompilerParams(
            collective_id=0, has_side_effects=True, vmem_limit_bytes=60 << 20
        ),
    )(
        near_target,
        order.reshape(-1),
        far_src.T,
        near_dest.reshape(-1, points),
        near_src.reshape(-1, points),
        order,
        right_side,
        basis,
        transfer,
        far_mats.reshape(-1, coeffs, coeffs),
        near_blocks,
    )
    first_x, first_z, second_x, second_z, second_u = (coefs[k, :, :1] for k in range(5))
    return (
        first_x * right_side + first_z * image,
        second_x * right_side + second_z * image + second_u * second,
    )


def solution(mesh):
    placed = (
        P(None, AXES),
        P(AXES, None, None),
        P(AXES, None, None),
        P(AXES, None),
        P(AXES, None),
        P(AXES, None, None, None),
        P(AXES),
        P(AXES, None),
        P(AXES),
        P(AXES, None, None),
    )
    return jax.shard_map(
        local,
        mesh=mesh,
        in_specs=placed,
        out_specs=(P(None, AXES), P(None, AXES)),
        check_vma=False,
    )
```

```python
import functools

import jax
import jax.numpy as jnp
from jax import lax
from jax.experimental import pallas as pl
from jax.experimental.pallas import tpu as pltpu
from jax.sharding import PartitionSpec as P

CHILDREN = 4
CAPACITY = 4
EPSILON = 1e-06
SCALE = 2.0**-20
STRIDE = 37
BLOCK = 16
GREET = 18
SPLIT = 96
TEAM = 16
AXES = ("leaf", "level")
LOGICAL = pl.DeviceIdType.LOGICAL
F32 = jnp.float32
BF16 = jnp.bfloat16


def combine(dots):
    start_sq = dots[0] + EPSILON
    start_norm = jnp.sqrt(start_sq)
    xx, xzs, zzs, xu, zu, uu = (dots[k] / start_sq for k in range(6))
    xz = xzs / SCALE
    zz = zzs / (SCALE * SCALE)
    along_one = 0.5 * xx + xz
    kappa = along_one - 0.5
    rest_raw = zz - 2.0 * kappa * xz + kappa * kappa * xx
    rest_sq = rest_raw + EPSILON
    rest_one = jnp.sqrt(rest_sq)
    scaled_rest = SCALE * rest_one
    scaled_sq = scaled_rest * scaled_rest
    beta = (xz - kappa * xx) / rest_one
    gamma = rest_raw / rest_sq
    one_t = (xu - kappa * xzs) / scaled_rest
    two_t = (zu - kappa * zzs - SCALE * kappa * (xu - kappa * xzs)) / scaled_sq
    t_t = (uu - 2.0 * kappa * zu + kappa * kappa * zzs) / scaled_sq
    cross_two = 0.5 * beta + one_t
    along_two = 0.5 * gamma + two_t
    short = 0.5 - along_two
    tail_sq = (
        t_t
        + short * short * gamma
        + cross_two * cross_two * xx
        + 2.0 * short * two_t
        - 2.0 * cross_two * one_t
        - 2.0 * cross_two * short * beta
    )
    gram_first = along_one * along_one + rest_one * rest_one
    gram_cross = along_one * cross_two + rest_one * along_two
    gram_last = cross_two * cross_two + along_two * along_two + tail_sq
    determinant = gram_first * gram_last - gram_cross * gram_cross
    coef_one = start_norm * (along_one * gram_last - cross_two * gram_cross) / determinant
    coef_two = start_norm * (gram_first * cross_two - gram_cross * along_one) / determinant
    one = coef_one / start_norm
    two = coef_two / (start_norm * rest_one)
    scaled_two = coef_two / (start_norm * scaled_rest)
    return (
        one - kappa * two,
        scaled_two,
        1.0 - 0.5 * one + 0.5 * kappa * two,
        -one / SCALE - (0.5 - kappa) * scaled_two,
        -scaled_two,
    )


def loop(count, unroll, body):
    def step(block, carry):
        for u in range(unroll):
            body(block * unroll + u)
        return carry

    lax.fori_loop(0, count // unroll, step, 0)


def send_tables(me, greet, dest, source, order, slots, labels):
    size = order.shape[1]
    lane = lax.broadcasted_iota(jnp.int32, (size, size), 1)
    row = lax.broadcasted_iota(jnp.int32, (size, size), 0)

    def upright(values):
        return jnp.sum(jnp.where(lane == row, values, 0), axis=1, keepdims=True)

    halves = dest.shape[0]
    dest_row = [dest[h : h + 1, :] for h in range(halves)]
    dest_col = [upright(values) for values in dest_row]
    source_col = [upright(source[h : h + 1, :]) for h in range(halves)]

    def turn_of(group):
        return ((group - me + size) * pow(STRIDE, -1, size) + size - 1) % size

    turn_row = [turn_of(values) for values in dest_row]
    turn_col = [turn_of(values) for values in dest_col]
    greet()
    rank = []
    place = []
    for h in range(halves):
        total = jnp.zeros((size, 1), jnp.int32)
        count = jnp.zeros((size, size), jnp.int32)
        for g in range(halves):
            count = count + jnp.where(turn_row[g] < turn_col[h], 1, 0)
            if g > h:
                continue
            same = dest_col[h] == dest_row[g]
            if g == h:
                same = same & (lane < row)
            total = total + jnp.sum(jnp.where(same, 1, 0), axis=1, keepdims=True)
        rank.append(total)
        greet()
        place.append(total + jnp.sum(count, axis=1, keepdims=True))
    every = []
    for k in range(CAPACITY):
        pair = jnp.zeros((1, size), jnp.int32)
        label = jnp.full((1, size), size, jnp.int32)
        for h in range(halves):
            chosen = (dest_col[h] == lane) & (rank[h] == k)
            pair = pair + jnp.sum(jnp.where(chosen, place[h], 0), axis=0, keepdims=True)
            label = label + jnp.sum(
                jnp.where(chosen, source_col[h] - size, 0), axis=0, keepdims=True
            )
        slots[pl.ds(k, 1), :] = pair
        every.append(label)
        greet()
    inverse = jnp.sum(jnp.where(upright(order) == lane, row, 0), axis=0, keepdims=True)
    slots[pl.ds(CAPACITY, 1), :] = jnp.minimum(inverse, size - 1)
    for b in range(halves):
        pair = jnp.zeros((1, size), jnp.int32)
        for h in range(halves):
            pair = pair + jnp.sum(
                jnp.where(place[h] == lane + b * size, row + h * size, 0), axis=0, keepdims=True
            )
        slots[pl.ds(CAPACITY + 1 + b, 1), :] = pair
    mixed = jnp.zeros((size, size), jnp.int32)
    for k in range(CAPACITY):
        mixed = jnp.where(lane == k, upright(every[k]), mixed)
    labels[...] = mixed.astype(F32).reshape(labels.shape)


def land_tables(labels, out):
    size = labels.shape[0]
    lane = lax.broadcasted_iota(jnp.int32, (size, size), 1)
    row = lax.broadcasted_iota(jnp.int32, (size, size), 0)
    columns = [labels[:, k : k + 1] for k in range(CAPACITY)]
    rows = [
        jnp.sum(jnp.where(lane == row, columns[k], 0), axis=0, keepdims=True)
        for k in range(CAPACITY)
    ]
    upto = jnp.zeros((size, size), jnp.int32)
    some = jnp.zeros((size, size), jnp.int32)
    perm = [jnp.zeros((size, size), jnp.int32) for _ in range(CAPACITY)]
    first = [jnp.zeros((size, size), jnp.int32) for _ in range(CAPACITY)]
    for k in range(CAPACITY):
        less = jnp.zeros((size, size), jnp.int32)
        tied = jnp.zeros((size, size), jnp.int32)
        for j in range(CAPACITY):
            less = less + jnp.where(rows[j] < columns[k], 1, 0)
            if j < k:
                tied = tied + jnp.where(rows[j] == columns[k], 1, 0)
            elif j == k:
                tied = tied + jnp.where((rows[j] == columns[k]) & (lane < row), 1, 0)
        below = jnp.sum(less, axis=1, keepdims=True)
        place = below + jnp.sum(tied, axis=1, keepdims=True)
        upto = upto + jnp.where(columns[k] <= lane, 1, 0)
        some = some + jnp.where(columns[k] == lane, 1, 0)
        for b in range(CAPACITY):
            here = place == lane + b * size
            perm[b] = perm[b] + jnp.where(here, CAPACITY * row + k, 0)
            first[b] = first[b] + jnp.where(here, below, 0)
    for b in range(CAPACITY):
        out[pl.ds(b, 1), :] = jnp.sum(perm[b], axis=0, keepdims=True)
        start = jnp.sum(first[b], axis=0, keepdims=True)
        out[pl.ds(CAPACITY + b, 1), :] = jnp.where(start == lane[0:1] + b * size, 0, 1)
    ends = jnp.sum(upto, axis=0, keepdims=True) - 1
    out[pl.ds(2 * CAPACITY, 1), :] = jnp.where(
        jnp.sum(some, axis=0, keepdims=True) > 0, ends, CAPACITY * size
    )


def kernel(
    target_ref, order_ref, far_ref,
    dest_ref, source_ref, order_row,
    x_hbm, basis_hbm, transfer_hbm, far_hbm, near_hbm,
    z_ref, u_ref, coef_ref,
    x_ref, basis_ref, transfer_ref, product_ref, turned_ref, far_w, near_w,
    part_ref, field_ref, run_ref, expansion_ref,
    up_send, up_recv, down_send, near_send,
    table_one, table_two, down_one, down_two, near_one, near_two, cast_one, cast_two,
    dot_send, dot_recv, label_send, label_recv,
    slot_rows, land_rows, slot_of, land_of,
    load_sem, table_sem, remote_sem,
):
    clusters = basis_ref.shape[0]
    devices = clusters
    levels = lax.axis_size("level")
    leaf, level = lax.axis_index("leaf"), lax.axis_index("level")
    leaves = devices // levels
    me = leaf * levels + level
    pairs = near_w.shape[0]
    parents = clusters // CHILDREN
    partners = far_w.shape[0] // parents
    lanes = basis_ref.shape[1]
    systems = x_ref.shape[0]
    chunks = 4
    rows = clusters // chunks

    load_x = pltpu.make_async_copy(x_hbm, x_ref, load_sem.at[0])
    def parts(src, dst, base):
        return [
            pltpu.make_async_copy(
                src.at[pl.ds(k * rows, rows)], dst.at[pl.ds(k * rows, rows)], load_sem.at[base + k]
            )
            for k in range(chunks)
        ]

    load_basis = parts(basis_hbm, basis_ref, 1)
    load_transfer = parts(transfer_hbm, transfer_ref, 1 + chunks)
    load_near = pltpu.make_async_copy(near_hbm, near_w, load_sem.at[1 + 2 * chunks])
    load_far = pltpu.make_async_copy(far_hbm, far_w, load_sem.at[2 + 2 * chunks])
    load_x.start()
    for copy in load_basis + load_transfer:
        copy.start()
    load_near.start()
    load_far.start()

    def peer(i):
        return (me + STRIDE * i) % devices

    barrier = pltpu.get_barrier_semaphore()

    greeted = [1]

    def greet():
        for i in range(greeted[0], min(greeted[0] + GREET, devices)):
            pl.semaphore_signal(barrier, inc=1, device_id=peer(i), device_id_type=LOGICAL)
        greeted[0] = min(greeted[0] + GREET, devices)

    def push(src, dst, stage, device):
        pltpu.make_async_remote_copy(
            src_ref=src,
            dst_ref=dst,
            send_sem=remote_sem.at[stage, 0],
            recv_sem=remote_sem.at[stage, 1],
            device_id=device,
            device_id_type=LOGICAL,
        ).start()

    sent = []

    def settle(ref, stage):
        pltpu.make_async_copy(ref, ref, remote_sem.at[stage, 1]).wait()
        sent.append(pltpu.make_async_copy(ref, ref, remote_sem.at[stage, 0]))

    def push_all(lo, hi, stage, src, dst):
        def go(i, carry):
            other = peer(i)
            push(src(other), dst, stage, other)
            return carry

        lax.fori_loop(lo, hi, go, 0, unroll=8)

    def tile(ref, c):
        return ref[:, pl.ds(pl.multiple_of(c * lanes, lanes), lanes)]

    send_tables(
        me, greet, dest_ref[...], source_ref[...], order_row[...], slot_rows, label_send
    )
    while greeted[0] < devices:
        greet()
    move_slots = pltpu.make_async_copy(slot_rows, slot_of, table_sem.at[0])
    move_slots.start()
    run_ref[CAPACITY * devices] = jnp.zeros(run_ref.shape[1:], F32)
    load_x.wait()
    for k in range(chunks):
        load_basis[k].wait()

        def expand(c, k=k):
            value = tile(x_ref, k * rows + c).astype(BF16)
            cast_one[k * rows + c] = value
            expansion_ref[k * rows + c] = jnp.dot(
                value, basis_ref[k * rows + c], preferred_element_type=F32
            ).astype(BF16)

        loop(rows, 32, expand)
    for copy in load_transfer:
        copy.wait()
    pl.semaphore_wait(barrier, devices - 1)

    zero = jnp.zeros((systems, lanes), F32)
    dots = []
    for trip in range(2):
        first = trip == 0
        stage = 4 * trip
        table_ref = table_one if first else table_two
        down_recv = down_one if first else down_two
        near_recv = near_one if first else near_two
        cast_ref = cast_one if first else cast_two

        before, matrix = (expansion_ref, transfer_ref) if first else (cast_two, product_ref)

        def lift(block):
            values = []
            for u in range(BLOCK):
                c = order_ref[peer(1 + block * BLOCK + u)]
                values.append(
                    jnp.dot(before[c], matrix[c], preferred_element_type=F32).astype(BF16)
                )
            return values

        def hold(block, values):
            for u in range(BLOCK):
                up_send[trip, peer(1 + block * BLOCK + u)] = values[u]

        def send_up(block, count):
            for u in range(count):
                other = peer(1 + block * BLOCK + u)
                push(up_send.at[trip, other], up_recv.at[trip, me], stage, other)

        hold(0, lift(0))

        def up(block, carry):
            values = lift(block)
            send_up(block - 1, BLOCK)
            hold(block, values)
            return carry

        blocks = devices // BLOCK
        lax.fori_loop(1, blocks, up, 0)
        send_up(blocks - 1, BLOCK - 1)
        up_recv[trip, me] = up_send[trip, me]

        if first:
            load_near.wait()

        if first:
            move_slots.wait()

        piece = pairs // CAPACITY

        def near_product(b):
            def one(j):
                n = slot_of[CAPACITY + 1 + b * piece // lanes, b * piece % lanes + j]
                part_ref[b * piece + j] = jnp.dot(
                    cast_ref[target_ref[n]], near_w[n], preferred_element_type=F32
                )

            loop(piece, 32, one)

        def near_push(lo, hi):
            def fill(i, carry):
                d = peer(i)
                for k in range(CAPACITY):
                    near_send[trip, CAPACITY * d + k] = part_ref[slot_of[k, d]].astype(BF16)
                return carry

            lax.fori_loop(lo, hi, fill, 0, unroll=4)
            push_all(
                lo,
                hi,
                stage + 3,
                lambda e: near_send.at[trip, pl.ds(CAPACITY * e, CAPACITY)],
                near_recv.at[pl.ds(CAPACITY * me, CAPACITY)],
            )

        step = piece // CAPACITY
        near_product(0)
        near_product(1)
        near_push(1, 1 + 2 * step)
        settle(up_recv.at[trip, pl.ds(0, devices - 1)], stage)

        def gather_parent(q):
            total = up_recv[trip, CHILDREN * q].astype(F32)
            for i in range(1, CHILDREN):
                total = total + up_recv[trip, CHILDREN * q + i].astype(F32)
            table_ref[level * parents + q] = total.astype(BF16)

        loop(parents, 8, gather_parent)
        mine = table_ref.at[pl.ds(level * parents, parents)]
        for i in range(1, CHILDREN):
            push(mine, mine, stage + 1, leaf * levels + (level + i) % levels)
        near_product(2)
        near_product(3)
        near_push(1 + 2 * step, SPLIT)
        if first:
            label_recv[pl.ds(me, 1)] = label_send[pl.ds(me, 1)]
            push_all(1, devices, 9, lambda e: label_send.at[e], label_recv.at[me])

            def fuse(c):
                value = jnp.dot(
                    basis_ref[c], transfer_ref[c], preferred_element_type=F32
                ).astype(BF16)
                product_ref[c] = value
                turned_ref[c] = value.T

            loop(clusters, 8, fuse)
            load_far.wait()
        settle(table_ref.at[pl.ds(0, (levels - 1) * parents)], stage + 1)

        def parent_of(j):
            return (leaf + 13 * j) % leaves

        group = BLOCK // levels

        def translate(block):
            values = []
            for u in range(group):
                q = parent_of(1 + block * group + u)
                picked = jnp.concatenate(
                    [table_ref[far_ref[k, q]] for k in range(partners)], axis=1
                )
                mats = far_w[pl.ds(partners * q, partners)].reshape(partners * lanes, lanes)
                values.append(jnp.dot(picked, mats, preferred_element_type=F32).astype(BF16))
            return values

        def keep(block, values):
            for u in range(group):
                down_send[trip, parent_of(1 + block * group + u)] = values[u]

        def send_down(block, last):
            for u in range(group):
                q = parent_of(1 + block * group + u)
                for i in range(1 if last and u == group - 1 else 0, levels):
                    other = q * levels + (level + i) % levels
                    push(down_send.at[trip, q], down_recv.at[me], stage + 2, other)

        keep(0, translate(0))

        def down(block, carry):
            values = translate(block)
            send_down(block - 1, False)
            keep(block, values)
            return carry

        lax.fori_loop(1, blocks, down, 0)
        send_down(blocks - 1, True)
        down_recv[me] = down_send[trip, leaf]
        near_push(SPLIT, devices)
        for k in range(CAPACITY):
            near_recv[CAPACITY * me + k] = part_ref[slot_of[k, me]].astype(BF16)
        if first:
            settle(label_recv.at[pl.ds(0, devices - 1)], 9)
            land_tables(
                label_recv[...].reshape(devices, lanes).astype(jnp.int32), land_rows
            )
            move_land = pltpu.make_async_copy(land_rows, land_of, table_sem.at[1])
            move_land.start()
            move_land.wait()
        settle(down_recv.at[pl.ds(0, devices - 1)], stage + 2)

        def spread(c):
            field_ref[c] = jnp.dot(
                down_recv[slot_of[CAPACITY, c]], turned_ref[c], preferred_element_type=F32
            )

        loop(clusters, 32, spread)
        settle(near_recv.at[pl.ds(0, CAPACITY * (devices - 1))], stage + 3)

        for b in range(CAPACITY):

            def land(block, total):
                for u in range(8):
                    i = block * 8 + u
                    total = total * land_of[CAPACITY + b, i].astype(F32) + near_recv[
                        land_of[b, i]
                    ].astype(F32)
                    run_ref[b * devices + i] = total
                return total

            total = lax.fori_loop(0, devices // 8, land, zero if b == 0 else total)

        def finish(block, sums):
            sums = list(sums)
            for u in range(8):
                c = block * 8 + u
                where = pl.ds(pl.multiple_of(c * lanes, lanes), lanes)
                value = field_ref[c] + run_ref[land_of[2 * CAPACITY, c]]
                x = x_ref[:, where]
                if first:
                    value = value * SCALE
                    z_ref[:, where] = value
                    cast_two[c] = value.astype(BF16)
                    terms = ((x, x), (x, value), (value, value))
                else:
                    u_ref[:, where] = value
                    terms = ((x, value), (z_ref[:, where], value), (value, value))
                for k, (p, q) in enumerate(terms):
                    sums[k] = sums[k] + p * q
            return tuple(sums)

        dots += lax.fori_loop(0, clusters // 8, finish, (zero,) * 3)

    lane = lax.broadcasted_iota(jnp.int32, (systems, lanes), 1)
    row = lax.broadcasted_iota(jnp.int32, (systems, lanes), 0)
    packed = zero
    for k, total in enumerate(dots):
        packed = jnp.where(
            lane == row + k * systems, jnp.sum(total, axis=1, keepdims=True), packed
        )
    packed = jnp.sum(packed, axis=0, keepdims=True)
    teams = devices // TEAM
    team, member = me // TEAM, me % TEAM
    dot_send[0] = packed
    dot_recv[pl.ds(member, 1)] = packed[None]
    for i in range(1, TEAM):
        push(dot_send.at[0], dot_recv.at[member], 8, team * TEAM + (member + i) % TEAM)
    settle(dot_recv.at[pl.ds(0, TEAM - 1)], 8)
    packed = jnp.sum(dot_recv[pl.ds(0, TEAM)], axis=0)
    dot_send[1] = packed
    dot_recv[pl.ds(TEAM + team, 1)] = packed[None]
    for i in range(1, teams):
        push(dot_send.at[1], dot_recv.at[TEAM + team], 10, (me + TEAM * i) % devices)
    settle(dot_recv.at[pl.ds(TEAM, teams - 1)], 10)
    packed = jnp.sum(dot_recv[pl.ds(TEAM, teams)], axis=0)
    gathered = jnp.broadcast_to(packed, (systems, lanes))
    scalars = combine(
        [
            jnp.sum(jnp.where(lane == row + k * systems, gathered, 0.0), axis=1, keepdims=True)
            for k in range(len(dots))
        ]
    )
    for k, value in enumerate(scalars):
        coef_ref[k] = jnp.broadcast_to(value, (systems, lanes))
    for copy in sent:
        copy.wait()


def finish(coef_ref, x_ref, z_ref, u_ref, solved_ref, left_ref):
    first_x, first_z, second_x, second_z, second_u = (coef_ref[k] for k in range(5))
    lanes = coef_ref.shape[2]
    for c in range(x_ref.shape[1] // lanes):
        where = pl.ds(c * lanes, lanes)
        x, z, u = x_ref[:, where], z_ref[:, where], u_ref[:, where]
        solved_ref[:, where] = first_x * x + first_z * z
        left_ref[:, where] = second_x * x + second_z * z + second_u * u


def local(
    right_side,
    basis,
    transfer,
    order,
    far_src,
    far_mats,
    near_target,
    near_dest,
    near_src,
    near_blocks,
):
    systems, panels = right_side.shape
    clusters, points, coeffs = basis.shape
    devices = lax.axis_size(AXES)
    pairs = near_target.shape[0]
    parents = clusters // CHILDREN
    slots = CAPACITY * devices
    smem = pl.BlockSpec(memory_space=pltpu.SMEM)
    hbm = pl.BlockSpec(memory_space=pltpu.HBM)
    vmem = pl.BlockSpec(memory_space=pltpu.VMEM)
    field = jax.ShapeDtypeStruct((systems, panels), F32)
    cell = (systems, points)
    image, second, coefs = pl.pallas_call(
        kernel,
        name="gmres",
        out_shape=(field, field, jax.ShapeDtypeStruct((5, systems, points), F32)),
        in_specs=[smem] * 3 + [vmem] * 3 + [hbm] * 5,
        out_specs=(vmem, vmem, vmem),
        scratch_shapes=[
            pltpu.VMEM((systems, panels), F32),
            pltpu.VMEM(basis.shape, BF16),
            pltpu.VMEM(transfer.shape, BF16),
            pltpu.VMEM(basis.shape, BF16),
            pltpu.VMEM(basis.shape, BF16),
            pltpu.VMEM((parents * far_src.shape[1], coeffs, coeffs), BF16),
            pltpu.VMEM(near_blocks.shape, BF16),
            pltpu.VMEM((pairs, *cell), F32),
            pltpu.VMEM((clusters, *cell), F32),
            pltpu.VMEM((slots + 8, *cell), F32),
            pltpu.VMEM((clusters, *cell), BF16),
            pltpu.VMEM((2, clusters, *cell), BF16),
            pltpu.VMEM((2, clusters, *cell), BF16),
            pltpu.VMEM((2, parents, *cell), BF16),
            pltpu.VMEM((2, slots, *cell), BF16),
            pltpu.VMEM((CHILDREN * parents, *cell), BF16),
            pltpu.VMEM((CHILDREN * parents, *cell), BF16),
            pltpu.VMEM((clusters, *cell), BF16),
            pltpu.VMEM((clusters, *cell), BF16),
            pltpu.VMEM((slots, *cell), BF16),
            pltpu.VMEM((slots, *cell), BF16),
            pltpu.VMEM((clusters, *cell), BF16),
            pltpu.VMEM((clusters, *cell), BF16),
            pltpu.VMEM((2, 1, points), F32),
            pltpu.VMEM((TEAM + devices // TEAM, 1, points), F32),
            pltpu.VMEM((devices, 1, points), F32),
            pltpu.VMEM((devices, 1, points), F32),
            pltpu.VMEM((8, devices), jnp.int32),
            pltpu.VMEM((16, devices), jnp.int32),
            pltpu.SMEM((8, devices), jnp.int32),
            pltpu.SMEM((16, devices), jnp.int32),
            pltpu.SemaphoreType.DMA((11,)),
            pltpu.SemaphoreType.DMA((2,)),
            pltpu.SemaphoreType.DMA((11, 2)),
        ],
        compiler_params=pltpu.CompilerParams(
            collective_id=0, has_side_effects=True, vmem_limit_bytes=60 << 20
        ),
    )(
        near_target,
        order.reshape(-1),
        far_src.T,
        near_dest.reshape(-1, points),
        near_src.reshape(-1, points),
        order,
        right_side,
        basis,
        transfer,
        far_mats.reshape(-1, coeffs, coeffs),
        near_blocks,
    )
    block = pl.BlockSpec((systems, panels // 4), lambda i: (0, i))
    return pl.pallas_call(
        finish,
        name="outputs",
        grid=(4,),
        out_shape=(field, field),
        in_specs=[pl.BlockSpec((5, systems, points), lambda i: (0, 0, 0))] + [block] * 3,
        out_specs=(block, block),
        compiler_params=pltpu.CompilerParams(vmem_limit_bytes=60 << 20),
    )(coefs, right_side, image, second)


def solution(mesh):
    placed = (
        P(None, AXES),
        P(AXES, None, None),
        P(AXES, None, None),
        P(AXES, None),
        P(AXES, None),
        P(AXES, None, None, None),
        P(AXES),
        P(AXES, None),
        P(AXES),
        P(AXES, None, None),
    )
    return jax.shard_map(
        local,
        mesh=mesh,
        in_specs=placed,
        out_specs=(P(None, AXES), P(None, AXES)),
        check_vma=False,
    )
```

```python
import functools

import jax
import jax.numpy as jnp
from jax import lax
from jax.experimental import pallas as pl
from jax.experimental.pallas import tpu as pltpu
from jax.sharding import PartitionSpec as P

CHILDREN = 4
CAPACITY = 4
EPSILON = 1e-06
SCALE = 2.0**-20
STRIDE = 37
BLOCK = 16
GREET = 18
SPLIT = 96
TEAM = 16
AXES = ("leaf", "level")
LOGICAL = pl.DeviceIdType.LOGICAL
F32 = jnp.float32
BF16 = jnp.bfloat16


def combine(dots):
    start_sq = dots[0] + EPSILON
    start_norm = jnp.sqrt(start_sq)
    xx, xzs, zzs, xu, zu, uu = (dots[k] / start_sq for k in range(6))
    xz = xzs / SCALE
    zz = zzs / (SCALE * SCALE)
    along_one = 0.5 * xx + xz
    kappa = along_one - 0.5
    rest_raw = zz - 2.0 * kappa * xz + kappa * kappa * xx
    rest_sq = rest_raw + EPSILON
    rest_one = jnp.sqrt(rest_sq)
    scaled_rest = SCALE * rest_one
    scaled_sq = scaled_rest * scaled_rest
    beta = (xz - kappa * xx) / rest_one
    gamma = rest_raw / rest_sq
    one_t = (xu - kappa * xzs) / scaled_rest
    two_t = (zu - kappa * zzs - SCALE * kappa * (xu - kappa * xzs)) / scaled_sq
    t_t = (uu - 2.0 * kappa * zu + kappa * kappa * zzs) / scaled_sq
    cross_two = 0.5 * beta + one_t
    along_two = 0.5 * gamma + two_t
    short = 0.5 - along_two
    tail_sq = (
        t_t
        + short * short * gamma
        + cross_two * cross_two * xx
        + 2.0 * short * two_t
        - 2.0 * cross_two * one_t
        - 2.0 * cross_two * short * beta
    )
    gram_first = along_one * along_one + rest_one * rest_one
    gram_cross = along_one * cross_two + rest_one * along_two
    gram_last = cross_two * cross_two + along_two * along_two + tail_sq
    determinant = gram_first * gram_last - gram_cross * gram_cross
    coef_one = start_norm * (along_one * gram_last - cross_two * gram_cross) / determinant
    coef_two = start_norm * (gram_first * cross_two - gram_cross * along_one) / determinant
    one = coef_one / start_norm
    two = coef_two / (start_norm * rest_one)
    scaled_two = coef_two / (start_norm * scaled_rest)
    return (
        one - kappa * two,
        scaled_two,
        1.0 - 0.5 * one + 0.5 * kappa * two,
        -one / SCALE - (0.5 - kappa) * scaled_two,
        -scaled_two,
    )


def loop(count, unroll, body):
    def step(block, carry):
        for u in range(unroll):
            body(block * unroll + u)
        return carry

    lax.fori_loop(0, count // unroll, step, 0)


def send_tables(me, greet, dest, source, order, slots, labels):
    size = order.shape[1]
    lane = lax.broadcasted_iota(jnp.int32, (size, size), 1)
    row = lax.broadcasted_iota(jnp.int32, (size, size), 0)

    def upright(values):
        return jnp.sum(jnp.where(lane == row, values, 0), axis=1, keepdims=True)

    halves = dest.shape[0]
    dest_row = [dest[h : h + 1, :] for h in range(halves)]
    dest_col = [upright(values) for values in dest_row]
    source_col = [upright(source[h : h + 1, :]) for h in range(halves)]

    def turn_of(group):
        return ((group - me + size) * pow(STRIDE, -1, size) + size - 1) % size

    turn_row = [turn_of(values) for values in dest_row]
    turn_col = [turn_of(values) for values in dest_col]
    greet()
    rank = []
    place = []
    for h in range(halves):
        total = jnp.zeros((size, 1), jnp.int32)
        count = jnp.zeros((size, size), jnp.int32)
        for g in range(halves):
            count = count + jnp.where(turn_row[g] < turn_col[h], 1, 0)
            if g > h:
                continue
            same = dest_col[h] == dest_row[g]
            if g == h:
                same = same & (lane < row)
            total = total + jnp.sum(jnp.where(same, 1, 0), axis=1, keepdims=True)
        rank.append(total)
        greet()
        place.append(total + jnp.sum(count, axis=1, keepdims=True))
    every = []
    for k in range(CAPACITY):
        pair = jnp.zeros((1, size), jnp.int32)
        label = jnp.full((1, size), size, jnp.int32)
        for h in range(halves):
            chosen = (dest_col[h] == lane) & (rank[h] == k)
            pair = pair + jnp.sum(jnp.where(chosen, place[h], 0), axis=0, keepdims=True)
            label = label + jnp.sum(
                jnp.where(chosen, source_col[h] - size, 0), axis=0, keepdims=True
            )
        slots[pl.ds(k, 1), :] = pair
        every.append(label)
        greet()
    inverse = jnp.sum(jnp.where(upright(order) == lane, row, 0), axis=0, keepdims=True)
    slots[pl.ds(CAPACITY, 1), :] = jnp.minimum(inverse, size - 1)
    for b in range(halves):
        pair = jnp.zeros((1, size), jnp.int32)
        for h in range(halves):
            pair = pair + jnp.sum(
                jnp.where(place[h] == lane + b * size, row + h * size, 0), axis=0, keepdims=True
            )
        slots[pl.ds(CAPACITY + 1 + b, 1), :] = pair
    mixed = jnp.zeros((size, size), jnp.int32)
    for k in range(CAPACITY):
        mixed = jnp.where(lane == k, upright(every[k]), mixed)
    labels[...] = mixed.astype(F32).reshape(labels.shape)


def land_tables(labels, out):
    size = labels.shape[0]
    lane = lax.broadcasted_iota(jnp.int32, (size, size), 1)
    row = lax.broadcasted_iota(jnp.int32, (size, size), 0)
    columns = [labels[:, k : k + 1] for k in range(CAPACITY)]
    rows = [
        jnp.sum(jnp.where(lane == row, columns[k], 0), axis=0, keepdims=True)
        for k in range(CAPACITY)
    ]
    upto = jnp.zeros((size, size), jnp.int32)
    some = jnp.zeros((size, size), jnp.int32)
    perm = [jnp.zeros((size, size), jnp.int32) for _ in range(CAPACITY)]
    first = [jnp.zeros((size, size), jnp.int32) for _ in range(CAPACITY)]
    for k in range(CAPACITY):
        less = jnp.zeros((size, size), jnp.int32)
        tied = jnp.zeros((size, size), jnp.int32)
        for j in range(CAPACITY):
            less = less + jnp.where(rows[j] < columns[k], 1, 0)
            if j < k:
                tied = tied + jnp.where(rows[j] == columns[k], 1, 0)
            elif j == k:
                tied = tied + jnp.where((rows[j] == columns[k]) & (lane < row), 1, 0)
        below = jnp.sum(less, axis=1, keepdims=True)
        place = below + jnp.sum(tied, axis=1, keepdims=True)
        upto = upto + jnp.where(columns[k] <= lane, 1, 0)
        some = some + jnp.where(columns[k] == lane, 1, 0)
        for b in range(CAPACITY):
            here = place == lane + b * size
            perm[b] = perm[b] + jnp.where(here, CAPACITY * row + k, 0)
            first[b] = first[b] + jnp.where(here, below, 0)
    for b in range(CAPACITY):
        out[pl.ds(b, 1), :] = jnp.sum(perm[b], axis=0, keepdims=True)
        start = jnp.sum(first[b], axis=0, keepdims=True)
        out[pl.ds(CAPACITY + b, 1), :] = jnp.where(start == lane[0:1] + b * size, 0, 1)
    ends = jnp.sum(upto, axis=0, keepdims=True) - 1
    out[pl.ds(2 * CAPACITY, 1), :] = jnp.where(
        jnp.sum(some, axis=0, keepdims=True) > 0, ends, CAPACITY * size
    )


def kernel(
    target_ref, order_ref, far_ref,
    dest_ref, source_ref, order_row,
    x_hbm, basis_hbm, transfer_hbm, far_hbm, near_hbm,
    z_hbm, u_hbm, coef_ref,
    z_ref, u_ref, x_ref, basis_ref, transfer_ref, product_ref, turned_ref, far_w, near_w,
    part_ref, field_ref, run_ref, expansion_ref,
    up_send, up_recv, down_send, near_send,
    table_one, table_two, down_one, down_two, near_one, near_two, cast_one, cast_two,
    dot_send, dot_recv, label_send, label_recv,
    slot_rows, land_rows, slot_of, land_of,
    load_sem, table_sem, remote_sem,
):
    clusters = basis_ref.shape[0]
    devices = clusters
    levels = lax.axis_size("level")
    leaf, level = lax.axis_index("leaf"), lax.axis_index("level")
    leaves = devices // levels
    me = leaf * levels + level
    pairs = near_w.shape[0]
    parents = clusters // CHILDREN
    partners = far_w.shape[0] // parents
    lanes = basis_ref.shape[1]
    systems = x_ref.shape[0]
    chunks = 4
    rows = clusters // chunks

    load_x = pltpu.make_async_copy(x_hbm, x_ref, load_sem.at[0])
    def parts(src, dst, base):
        return [
            pltpu.make_async_copy(
                src.at[pl.ds(k * rows, rows)], dst.at[pl.ds(k * rows, rows)], load_sem.at[base + k]
            )
            for k in range(chunks)
        ]

    load_basis = parts(basis_hbm, basis_ref, 1)
    load_transfer = parts(transfer_hbm, transfer_ref, 1 + chunks)
    load_near = pltpu.make_async_copy(near_hbm, near_w, load_sem.at[1 + 2 * chunks])
    load_far = pltpu.make_async_copy(far_hbm, far_w, load_sem.at[2 + 2 * chunks])
    load_x.start()
    for copy in load_basis + load_transfer:
        copy.start()
    load_near.start()
    load_far.start()

    def peer(i):
        return (me + STRIDE * i) % devices

    barrier = pltpu.get_barrier_semaphore()

    greeted = [1]

    def greet():
        for i in range(greeted[0], min(greeted[0] + GREET, devices)):
            pl.semaphore_signal(barrier, inc=1, device_id=peer(i), device_id_type=LOGICAL)
        greeted[0] = min(greeted[0] + GREET, devices)

    def push(src, dst, stage, device):
        pltpu.make_async_remote_copy(
            src_ref=src,
            dst_ref=dst,
            send_sem=remote_sem.at[stage, 0],
            recv_sem=remote_sem.at[stage, 1],
            device_id=device,
            device_id_type=LOGICAL,
        ).start()

    sent = []

    def settle(ref, stage):
        pltpu.make_async_copy(ref, ref, remote_sem.at[stage, 1]).wait()
        sent.append(pltpu.make_async_copy(ref, ref, remote_sem.at[stage, 0]))

    def push_all(lo, hi, stage, src, dst):
        def go(i, carry):
            other = peer(i)
            push(src(other), dst, stage, other)
            return carry

        lax.fori_loop(lo, hi, go, 0, unroll=8)

    def tile(ref, c):
        return ref[:, pl.ds(pl.multiple_of(c * lanes, lanes), lanes)]

    send_tables(
        me, greet, dest_ref[...], source_ref[...], order_row[...], slot_rows, label_send
    )
    while greeted[0] < devices:
        greet()
    move_slots = pltpu.make_async_copy(slot_rows, slot_of, table_sem.at[0])
    move_slots.start()
    run_ref[CAPACITY * devices] = jnp.zeros(run_ref.shape[1:], F32)
    load_x.wait()
    for k in range(chunks):
        load_basis[k].wait()

        def expand(c, k=k):
            value = tile(x_ref, k * rows + c).astype(BF16)
            cast_one[k * rows + c] = value
            expansion_ref[k * rows + c] = jnp.dot(
                value, basis_ref[k * rows + c], preferred_element_type=F32
            ).astype(BF16)

        loop(rows, 32, expand)
    for copy in load_transfer:
        copy.wait()
    piece = pairs // CAPACITY

    def near_product(field, b):
        def one(j):
            n = slot_of[CAPACITY + 1 + b * piece // lanes, b * piece % lanes + j]
            part_ref[b * piece + j] = jnp.dot(
                field[target_ref[n]], near_w[n], preferred_element_type=F32
            )

        loop(piece, 32, one)

    move_slots.wait()
    pl.semaphore_wait(barrier, devices - 1)

    zero = jnp.zeros((systems, lanes), F32)
    dots = []
    for trip in range(2):
        first = trip == 0
        stage = 4 * trip
        table_ref = table_one if first else table_two
        down_recv = down_one if first else down_two
        near_recv = near_one if first else near_two
        cast_ref = cast_one if first else cast_two

        before, matrix = (expansion_ref, transfer_ref) if first else (cast_two, product_ref)

        def lift(block):
            values = []
            for u in range(BLOCK):
                c = order_ref[peer(1 + block * BLOCK + u)]
                values.append(
                    jnp.dot(before[c], matrix[c], preferred_element_type=F32).astype(BF16)
                )
            return values

        def hold(block, values):
            for u in range(BLOCK):
                up_send[trip, peer(1 + block * BLOCK + u)] = values[u]

        def send_up(block, count):
            for u in range(count):
                other = peer(1 + block * BLOCK + u)
                push(up_send.at[trip, other], up_recv.at[trip, me], stage, other)

        hold(0, lift(0))

        def up(block, carry):
            values = lift(block)
            send_up(block - 1, BLOCK)
            hold(block, values)
            return carry

        blocks = devices // BLOCK
        lax.fori_loop(1, blocks, up, 0)
        send_up(blocks - 1, BLOCK - 1)
        up_recv[trip, me] = up_send[trip, me]
        if first:
            load_near.wait()

        def near_push(lo, hi):
            def fill(i, carry):
                d = peer(i)
                for k in range(CAPACITY):
                    near_send[trip, CAPACITY * d + k] = part_ref[slot_of[k, d]].astype(BF16)
                return carry

            lax.fori_loop(lo, hi, fill, 0, unroll=4)
            push_all(
                lo,
                hi,
                stage + 3,
                lambda e: near_send.at[trip, pl.ds(CAPACITY * e, CAPACITY)],
                near_recv.at[pl.ds(CAPACITY * me, CAPACITY)],
            )

        step = piece // CAPACITY
        for b in range(2):
            near_product(cast_ref, b)
        near_push(1, 1 + 2 * step)
        settle(up_recv.at[trip, pl.ds(0, devices - 1)], stage)

        def gather_parent(q):
            total = up_recv[trip, CHILDREN * q].astype(F32)
            for i in range(1, CHILDREN):
                total = total + up_recv[trip, CHILDREN * q + i].astype(F32)
            table_ref[level * parents + q] = total.astype(BF16)

        loop(parents, 8, gather_parent)
        mine = table_ref.at[pl.ds(level * parents, parents)]
        for i in range(1, CHILDREN):
            push(mine, mine, stage + 1, leaf * levels + (level + i) % levels)
        for b in range(2, CAPACITY):
            near_product(cast_ref, b)
        near_push(1 + 2 * step, SPLIT)
        if first:
            label_recv[pl.ds(me, 1)] = label_send[pl.ds(me, 1)]
            push_all(1, devices, 9, lambda e: label_send.at[e], label_recv.at[me])

            def fuse(c):
                value = jnp.dot(
                    basis_ref[c], transfer_ref[c], preferred_element_type=F32
                ).astype(BF16)
                product_ref[c] = value
                turned_ref[c] = value.T

            loop(clusters, 8, fuse)
            load_far.wait()
        settle(table_ref.at[pl.ds(0, (levels - 1) * parents)], stage + 1)

        def parent_of(j):
            return (leaf + 13 * j) % leaves

        group = BLOCK // levels

        def translate(block):
            values = []
            for u in range(group):
                q = parent_of(1 + block * group + u)
                picked = jnp.concatenate(
                    [table_ref[far_ref[k, q]] for k in range(partners)], axis=1
                )
                mats = far_w[pl.ds(partners * q, partners)].reshape(partners * lanes, lanes)
                values.append(jnp.dot(picked, mats, preferred_element_type=F32).astype(BF16))
            return values

        def keep(block, values):
            for u in range(group):
                down_send[trip, parent_of(1 + block * group + u)] = values[u]

        def send_down(block, last):
            for u in range(group):
                q = parent_of(1 + block * group + u)
                for i in range(1 if last and u == group - 1 else 0, levels):
                    other = q * levels + (level + i) % levels
                    push(down_send.at[trip, q], down_recv.at[me], stage + 2, other)

        keep(0, translate(0))

        def down(block, carry):
            values = translate(block)
            send_down(block - 1, False)
            keep(block, values)
            return carry

        lax.fori_loop(1, blocks, down, 0)
        send_down(blocks - 1, True)
        down_recv[me] = down_send[trip, leaf]
        near_push(SPLIT, devices)
        for k in range(CAPACITY):
            near_recv[CAPACITY * me + k] = part_ref[slot_of[k, me]].astype(BF16)
        if first:
            settle(label_recv.at[pl.ds(0, devices - 1)], 9)
            land_tables(
                label_recv[...].reshape(devices, lanes).astype(jnp.int32), land_rows
            )
            move_land = pltpu.make_async_copy(land_rows, land_of, table_sem.at[1])
            move_land.start()
            move_land.wait()
        settle(down_recv.at[pl.ds(0, devices - 1)], stage + 2)

        def spread(c):
            field_ref[c] = jnp.dot(
                down_recv[slot_of[CAPACITY, c]], turned_ref[c], preferred_element_type=F32
            )

        loop(clusters, 32, spread)
        settle(near_recv.at[pl.ds(0, CAPACITY * (devices - 1))], stage + 3)

        for b in range(CAPACITY):

            def land(block, total):
                for u in range(8):
                    i = block * 8 + u
                    total = total * land_of[CAPACITY + b, i].astype(F32) + near_recv[
                        land_of[b, i]
                    ].astype(F32)
                    run_ref[b * devices + i] = total
                return total

            total = lax.fori_loop(0, devices // 8, land, zero if b == 0 else total)

        def finish(block, sums):
            sums = list(sums)
            for u in range(8):
                c = block * 8 + u
                where = pl.ds(pl.multiple_of(c * lanes, lanes), lanes)
                value = field_ref[c] + run_ref[land_of[2 * CAPACITY, c]]
                x = x_ref[:, where]
                if first:
                    value = value * SCALE
                    z_ref[:, where] = value
                    cast_two[c] = value.astype(BF16)
                    terms = ((x, x), (x, value), (value, value))
                else:
                    u_ref[:, where] = value
                    terms = ((x, value), (z_ref[:, where], value), (value, value))
                for k, (p, q) in enumerate(terms):
                    sums[k] = sums[k] + p * q
            return tuple(sums)

        dots += lax.fori_loop(0, clusters // 8, finish, (zero,) * 3)
        store = pltpu.make_async_copy(
            z_ref if first else u_ref, z_hbm if first else u_hbm, table_sem.at[2 + trip]
        )
        store.start()
        sent.append(store)

    lane = lax.broadcasted_iota(jnp.int32, (systems, lanes), 1)
    row = lax.broadcasted_iota(jnp.int32, (systems, lanes), 0)
    packed = zero
    for k, total in enumerate(dots):
        packed = jnp.where(
            lane == row + k * systems, jnp.sum(total, axis=1, keepdims=True), packed
        )
    packed = jnp.sum(packed, axis=0, keepdims=True)
    teams = devices // TEAM
    team, member = me // TEAM, me % TEAM
    dot_send[0] = packed
    dot_recv[pl.ds(member, 1)] = packed[None]
    for i in range(1, TEAM):
        push(dot_send.at[0], dot_recv.at[member], 8, team * TEAM + (member + i) % TEAM)
    settle(dot_recv.at[pl.ds(0, TEAM - 1)], 8)
    packed = jnp.sum(dot_recv[pl.ds(0, TEAM)], axis=0)
    dot_send[1] = packed
    dot_recv[pl.ds(TEAM + team, 1)] = packed[None]
    for i in range(1, teams):
        push(dot_send.at[1], dot_recv.at[TEAM + team], 10, (me + TEAM * i) % devices)
    settle(dot_recv.at[pl.ds(TEAM, teams - 1)], 10)
    packed = jnp.sum(dot_recv[pl.ds(TEAM, teams)], axis=0)
    gathered = jnp.broadcast_to(packed, (systems, lanes))
    scalars = combine(
        [
            jnp.sum(jnp.where(lane == row + k * systems, gathered, 0.0), axis=1, keepdims=True)
            for k in range(len(dots))
        ]
    )
    for k, value in enumerate(scalars):
        coef_ref[k] = jnp.broadcast_to(value, (systems, lanes))
    for copy in sent:
        copy.wait()


def finish(coef_ref, x_ref, z_ref, u_ref, solved_ref, left_ref):
    first_x, first_z, second_x, second_z, second_u = (coef_ref[k] for k in range(5))
    lanes = coef_ref.shape[2]
    for c in range(x_ref.shape[1] // lanes):
        where = pl.ds(c * lanes, lanes)
        x, z, u = x_ref[:, where], z_ref[:, where], u_ref[:, where]
        solved_ref[:, where] = first_x * x + first_z * z
        left_ref[:, where] = second_x * x + second_z * z + second_u * u


def local(
    right_side,
    basis,
    transfer,
    order,
    far_src,
    far_mats,
    near_target,
    near_dest,
    near_src,
    near_blocks,
):
    systems, panels = right_side.shape
    clusters, points, coeffs = basis.shape
    devices = lax.axis_size(AXES)
    pairs = near_target.shape[0]
    parents = clusters // CHILDREN
    slots = CAPACITY * devices
    smem = pl.BlockSpec(memory_space=pltpu.SMEM)
    hbm = pl.BlockSpec(memory_space=pltpu.HBM)
    vmem = pl.BlockSpec(memory_space=pltpu.VMEM)
    field = jax.ShapeDtypeStruct((systems, panels), F32)
    cell = (systems, points)
    image, second, coefs = pl.pallas_call(
        kernel,
        name="gmres",
        out_shape=(field, field, jax.ShapeDtypeStruct((5, systems, points), F32)),
        in_specs=[smem] * 3 + [vmem] * 3 + [hbm] * 5,
        out_specs=(hbm, hbm, vmem),
        scratch_shapes=[
            pltpu.VMEM((systems, panels), F32),
            pltpu.VMEM((systems, panels), F32),
            pltpu.VMEM((systems, panels), F32),
            pltpu.VMEM(basis.shape, BF16),
            pltpu.VMEM(transfer.shape, BF16),
            pltpu.VMEM(basis.shape, BF16),
            pltpu.VMEM(basis.shape, BF16),
            pltpu.VMEM((parents * far_src.shape[1], coeffs, coeffs), BF16),
            pltpu.VMEM(near_blocks.shape, BF16),
            pltpu.VMEM((pairs, *cell), F32),
            pltpu.VMEM((clusters, *cell), F32),
            pltpu.VMEM((slots + 8, *cell), F32),
            pltpu.VMEM((clusters, *cell), BF16),
            pltpu.VMEM((2, clusters, *cell), BF16),
            pltpu.VMEM((2, clusters, *cell), BF16),
            pltpu.VMEM((2, parents, *cell), BF16),
            pltpu.VMEM((2, slots, *cell), BF16),
            pltpu.VMEM((CHILDREN * parents, *cell), BF16),
            pltpu.VMEM((CHILDREN * parents, *cell), BF16),
            pltpu.VMEM((clusters, *cell), BF16),
            pltpu.VMEM((clusters, *cell), BF16),
            pltpu.VMEM((slots, *cell), BF16),
            pltpu.VMEM((slots, *cell), BF16),
            pltpu.VMEM((clusters, *cell), BF16),
            pltpu.VMEM((clusters, *cell), BF16),
            pltpu.VMEM((2, 1, points), F32),
            pltpu.VMEM((TEAM + devices // TEAM, 1, points), F32),
            pltpu.VMEM((devices, 1, points), F32),
            pltpu.VMEM((devices, 1, points), F32),
            pltpu.VMEM((8, devices), jnp.int32),
            pltpu.VMEM((16, devices), jnp.int32),
            pltpu.SMEM((8, devices), jnp.int32),
            pltpu.SMEM((16, devices), jnp.int32),
            pltpu.SemaphoreType.DMA((11,)),
            pltpu.SemaphoreType.DMA((4,)),
            pltpu.SemaphoreType.DMA((11, 2)),
        ],
        compiler_params=pltpu.CompilerParams(
            collective_id=0, has_side_effects=True, vmem_limit_bytes=60 << 20
        ),
    )(
        near_target,
        order.reshape(-1),
        far_src.T,
        near_dest.reshape(-1, points),
        near_src.reshape(-1, points),
        order,
        right_side,
        basis,
        transfer,
        far_mats.reshape(-1, coeffs, coeffs),
        near_blocks,
    )
    block = pl.BlockSpec((systems, panels // 2), lambda i: (0, i))
    return pl.pallas_call(
        finish,
        name="outputs",
        grid=(2,),
        out_shape=(field, field),
        in_specs=[pl.BlockSpec((5, systems, points), lambda i: (0, 0, 0))] + [block] * 3,
        out_specs=(block, block),
        compiler_params=pltpu.CompilerParams(vmem_limit_bytes=60 << 20),
    )(coefs, right_side, image, second)


def solution(mesh):
    placed = (
        P(None, AXES),
        P(AXES, None, None),
        P(AXES, None, None),
        P(AXES, None),
        P(AXES, None),
        P(AXES, None, None, None),
        P(AXES),
        P(AXES, None),
        P(AXES),
        P(AXES, None, None),
    )
    return jax.shard_map(
        local,
        mesh=mesh,
        in_specs=placed,
        out_specs=(P(None, AXES), P(None, AXES)),
        check_vma=False,
    )
```

```python
import functools

import jax
import jax.numpy as jnp
from jax import lax
from jax.experimental import pallas as pl
from jax.experimental.pallas import tpu as pltpu
from jax.sharding import PartitionSpec as P

CHILDREN = 4
CAPACITY = 4
EPSILON = 1e-06
SCALE = 2.0**-20
STRIDE = 37
BLOCK = 32
GREET = 18
SPLIT = 96
TEAM = 16
AXES = ("leaf", "level")
LOGICAL = pl.DeviceIdType.LOGICAL
F32 = jnp.float32
BF16 = jnp.bfloat16


def combine(dots):
    start_sq = dots[0] + EPSILON
    start_norm = jnp.sqrt(start_sq)
    xx, xzs, zzs, xu, zu, uu = (dots[k] / start_sq for k in range(6))
    xz = xzs / SCALE
    zz = zzs / (SCALE * SCALE)
    along_one = 0.5 * xx + xz
    kappa = along_one - 0.5
    rest_raw = zz - 2.0 * kappa * xz + kappa * kappa * xx
    rest_sq = rest_raw + EPSILON
    rest_one = jnp.sqrt(rest_sq)
    scaled_rest = SCALE * rest_one
    scaled_sq = scaled_rest * scaled_rest
    beta = (xz - kappa * xx) / rest_one
    gamma = rest_raw / rest_sq
    one_t = (xu - kappa * xzs) / scaled_rest
    two_t = (zu - kappa * zzs - SCALE * kappa * (xu - kappa * xzs)) / scaled_sq
    t_t = (uu - 2.0 * kappa * zu + kappa * kappa * zzs) / scaled_sq
    cross_two = 0.5 * beta + one_t
    along_two = 0.5 * gamma + two_t
    short = 0.5 - along_two
    tail_sq = (
        t_t
        + short * short * gamma
        + cross_two * cross_two * xx
        + 2.0 * short * two_t
        - 2.0 * cross_two * one_t
        - 2.0 * cross_two * short * beta
    )
    gram_first = along_one * along_one + rest_one * rest_one
    gram_cross = along_one * cross_two + rest_one * along_two
    gram_last = cross_two * cross_two + along_two * along_two + tail_sq
    determinant = gram_first * gram_last - gram_cross * gram_cross
    coef_one = start_norm * (along_one * gram_last - cross_two * gram_cross) / determinant
    coef_two = start_norm * (gram_first * cross_two - gram_cross * along_one) / determinant
    one = coef_one / start_norm
    two = coef_two / (start_norm * rest_one)
    scaled_two = coef_two / (start_norm * scaled_rest)
    return (
        one - kappa * two,
        scaled_two,
        1.0 - 0.5 * one + 0.5 * kappa * two,
        -one / SCALE - (0.5 - kappa) * scaled_two,
        -scaled_two,
    )


def loop(count, unroll, body):
    def step(block, carry):
        for u in range(unroll):
            body(block * unroll + u)
        return carry

    lax.fori_loop(0, count // unroll, step, 0)


def send_tables(me, greet, dest, source, order, slots, labels):
    size = order.shape[1]
    lane = lax.broadcasted_iota(jnp.int32, (size, size), 1)
    row = lax.broadcasted_iota(jnp.int32, (size, size), 0)

    def upright(values):
        return jnp.sum(jnp.where(lane == row, values, 0), axis=1, keepdims=True)

    halves = dest.shape[0]
    dest_row = [dest[h : h + 1, :] for h in range(halves)]
    dest_col = [upright(values) for values in dest_row]
    source_col = [upright(source[h : h + 1, :]) for h in range(halves)]

    def turn_of(group):
        return ((group - me + size) * pow(STRIDE, -1, size) + size - 1) % size

    turn_row = [turn_of(values) for values in dest_row]
    turn_col = [turn_of(values) for values in dest_col]
    greet()
    rank = []
    place = []
    for h in range(halves):
        total = jnp.zeros((size, 1), jnp.int32)
        count = jnp.zeros((size, size), jnp.int32)
        for g in range(halves):
            count = count + jnp.where(turn_row[g] < turn_col[h], 1, 0)
            if g > h:
                continue
            same = dest_col[h] == dest_row[g]
            if g == h:
                same = same & (lane < row)
            total = total + jnp.sum(jnp.where(same, 1, 0), axis=1, keepdims=True)
        rank.append(total)
        greet()
        place.append(total + jnp.sum(count, axis=1, keepdims=True))
    every = []
    for k in range(CAPACITY):
        pair = jnp.zeros((1, size), jnp.int32)
        label = jnp.full((1, size), size, jnp.int32)
        for h in range(halves):
            chosen = (dest_col[h] == lane) & (rank[h] == k)
            pair = pair + jnp.sum(jnp.where(chosen, place[h], 0), axis=0, keepdims=True)
            label = label + jnp.sum(
                jnp.where(chosen, source_col[h] - size, 0), axis=0, keepdims=True
            )
        slots[pl.ds(k, 1), :] = pair
        every.append(label)
        greet()
    inverse = jnp.sum(jnp.where(upright(order) == lane, row, 0), axis=0, keepdims=True)
    slots[pl.ds(CAPACITY, 1), :] = jnp.minimum(inverse, size - 1)
    for b in range(halves):
        pair = jnp.zeros((1, size), jnp.int32)
        for h in range(halves):
            pair = pair + jnp.sum(
                jnp.where(place[h] == lane + b * size, row + h * size, 0), axis=0, keepdims=True
            )
        slots[pl.ds(CAPACITY + 1 + b, 1), :] = pair
    mixed = jnp.zeros((size, size), jnp.int32)
    for k in range(CAPACITY):
        mixed = jnp.where(lane == k, upright(every[k]), mixed)
    labels[...] = mixed.astype(F32).reshape(labels.shape)


def land_tables(labels, out):
    size = labels.shape[0]
    lane = lax.broadcasted_iota(jnp.int32, (size, size), 1)
    row = lax.broadcasted_iota(jnp.int32, (size, size), 0)
    columns = [labels[:, k : k + 1] for k in range(CAPACITY)]
    rows = [
        jnp.sum(jnp.where(lane == row, columns[k], 0), axis=0, keepdims=True)
        for k in range(CAPACITY)
    ]
    upto = jnp.zeros((size, size), jnp.int32)
    some = jnp.zeros((size, size), jnp.int32)
    perm = [jnp.zeros((size, size), jnp.int32) for _ in range(CAPACITY)]
    first = [jnp.zeros((size, size), jnp.int32) for _ in range(CAPACITY)]
    for k in range(CAPACITY):
        less = jnp.zeros((size, size), jnp.int32)
        tied = jnp.zeros((size, size), jnp.int32)
        for j in range(CAPACITY):
            less = less + jnp.where(rows[j] < columns[k], 1, 0)
            if j < k:
                tied = tied + jnp.where(rows[j] == columns[k], 1, 0)
            elif j == k:
                tied = tied + jnp.where((rows[j] == columns[k]) & (lane < row), 1, 0)
        below = jnp.sum(less, axis=1, keepdims=True)
        place = below + jnp.sum(tied, axis=1, keepdims=True)
        upto = upto + jnp.where(columns[k] <= lane, 1, 0)
        some = some + jnp.where(columns[k] == lane, 1, 0)
        for b in range(CAPACITY):
            here = place == lane + b * size
            perm[b] = perm[b] + jnp.where(here, CAPACITY * row + k, 0)
            first[b] = first[b] + jnp.where(here, below, 0)
    for b in range(CAPACITY):
        out[pl.ds(b, 1), :] = jnp.sum(perm[b], axis=0, keepdims=True)
        start = jnp.sum(first[b], axis=0, keepdims=True)
        out[pl.ds(CAPACITY + b, 1), :] = jnp.where(start == lane[0:1] + b * size, 0, 1)
    ends = jnp.sum(upto, axis=0, keepdims=True) - 1
    out[pl.ds(2 * CAPACITY, 1), :] = jnp.where(
        jnp.sum(some, axis=0, keepdims=True) > 0, ends, CAPACITY * size
    )


def kernel(
    target_ref, order_ref, far_ref,
    dest_ref, source_ref, order_row,
    x_hbm, basis_hbm, transfer_hbm, far_hbm, near_hbm,
    z_hbm, u_hbm, coef_ref,
    z_ref, u_ref, x_ref, basis_ref, transfer_ref, product_ref, turned_ref, far_w, near_w,
    part_ref, field_ref, run_ref, expansion_ref,
    up_send, up_recv, down_send, near_send,
    table_one, table_two, down_one, down_two, near_one, near_two, cast_one, cast_two,
    dot_send, dot_recv, label_send, label_recv,
    slot_rows, land_rows, slot_of, land_of,
    load_sem, table_sem, remote_sem,
):
    clusters = basis_ref.shape[0]
    devices = clusters
    levels = lax.axis_size("level")
    leaf, level = lax.axis_index("leaf"), lax.axis_index("level")
    leaves = devices // levels
    me = leaf * levels + level
    pairs = near_w.shape[0]
    parents = clusters // CHILDREN
    partners = far_w.shape[0] // parents
    lanes = basis_ref.shape[1]
    systems = x_ref.shape[0]
    chunks = 4
    rows = clusters // chunks

    load_x = pltpu.make_async_copy(x_hbm, x_ref, load_sem.at[0])
    def parts(src, dst, base):
        return [
            pltpu.make_async_copy(
                src.at[pl.ds(k * rows, rows)], dst.at[pl.ds(k * rows, rows)], load_sem.at[base + k]
            )
            for k in range(chunks)
        ]

    load_basis = parts(basis_hbm, basis_ref, 1)
    load_transfer = parts(transfer_hbm, transfer_ref, 1 + chunks)
    load_near = pltpu.make_async_copy(near_hbm, near_w, load_sem.at[1 + 2 * chunks])
    load_far = pltpu.make_async_copy(far_hbm, far_w, load_sem.at[2 + 2 * chunks])
    load_x.start()
    for copy in load_basis + load_transfer:
        copy.start()
    load_near.start()
    load_far.start()

    def peer(i):
        return (me + STRIDE * i) % devices

    barrier = pltpu.get_barrier_semaphore()

    greeted = [1]

    def greet():
        for i in range(greeted[0], min(greeted[0] + GREET, devices)):
            pl.semaphore_signal(barrier, inc=1, device_id=peer(i), device_id_type=LOGICAL)
        greeted[0] = min(greeted[0] + GREET, devices)

    def push(src, dst, stage, device):
        pltpu.make_async_remote_copy(
            src_ref=src,
            dst_ref=dst,
            send_sem=remote_sem.at[stage, 0],
            recv_sem=remote_sem.at[stage, 1],
            device_id=device,
            device_id_type=LOGICAL,
        ).start()

    sent = []

    def settle(ref, stage):
        pltpu.make_async_copy(ref, ref, remote_sem.at[stage, 1]).wait()
        sent.append(pltpu.make_async_copy(ref, ref, remote_sem.at[stage, 0]))

    def push_all(lo, hi, stage, src, dst):
        def go(i, carry):
            other = peer(i)
            push(src(other), dst, stage, other)
            return carry

        lax.fori_loop(lo, hi, go, 0, unroll=8)

    def tile(ref, c):
        return ref[:, pl.ds(pl.multiple_of(c * lanes, lanes), lanes)]

    send_tables(
        me, greet, dest_ref[...], source_ref[...], order_row[...], slot_rows, label_send
    )
    while greeted[0] < devices:
        greet()
    move_slots = pltpu.make_async_copy(slot_rows, slot_of, table_sem.at[0])
    move_slots.start()
    run_ref[CAPACITY * devices] = jnp.zeros(run_ref.shape[1:], F32)
    load_x.wait()
    for k in range(chunks):
        load_basis[k].wait()

        def expand(c, k=k):
            value = tile(x_ref, k * rows + c).astype(BF16)
            cast_one[k * rows + c] = value
            expansion_ref[k * rows + c] = jnp.dot(
                value, basis_ref[k * rows + c], preferred_element_type=F32
            ).astype(BF16)

        loop(rows, 32, expand)
    for copy in load_transfer:
        copy.wait()
    piece = pairs // CAPACITY

    def near_product(field, b):
        def one(j):
            n = slot_of[CAPACITY + 1 + b * piece // lanes, b * piece % lanes + j]
            part_ref[b * piece + j] = jnp.dot(
                field[target_ref[n]], near_w[n], preferred_element_type=F32
            )

        loop(piece, 32, one)

    move_slots.wait()
    pl.semaphore_wait(barrier, devices - 1)

    zero = jnp.zeros((systems, lanes), F32)
    dots = []
    for trip in range(2):
        first = trip == 0
        stage = 4 * trip
        table_ref = table_one if first else table_two
        down_recv = down_one if first else down_two
        near_recv = near_one if first else near_two
        cast_ref = cast_one if first else cast_two

        before, matrix = (expansion_ref, transfer_ref) if first else (cast_two, product_ref)

        def lift(block):
            values = []
            for u in range(BLOCK):
                c = order_ref[peer(1 + block * BLOCK + u)]
                values.append(
                    jnp.dot(before[c], matrix[c], preferred_element_type=F32).astype(BF16)
                )
            return values

        def hold(block, values):
            for u in range(BLOCK):
                up_send[trip, peer(1 + block * BLOCK + u)] = values[u]

        def send_up(block, count):
            for u in range(count):
                other = peer(1 + block * BLOCK + u)
                push(up_send.at[trip, other], up_recv.at[trip, me], stage, other)

        hold(0, lift(0))

        def up(block, carry):
            values = lift(block)
            send_up(block - 1, BLOCK)
            hold(block, values)
            return carry

        blocks = devices // BLOCK
        lax.fori_loop(1, blocks, up, 0)
        send_up(blocks - 1, BLOCK - 1)
        up_recv[trip, me] = up_send[trip, me]
        if first:
            load_near.wait()

        def near_push(lo, hi):
            def fill(i, carry):
                d = peer(i)
                for k in range(CAPACITY):
                    near_send[trip, CAPACITY * d + k] = part_ref[slot_of[k, d]].astype(BF16)
                return carry

            lax.fori_loop(lo, hi, fill, 0, unroll=4)
            push_all(
                lo,
                hi,
                stage + 3,
                lambda e: near_send.at[trip, pl.ds(CAPACITY * e, CAPACITY)],
                near_recv.at[pl.ds(CAPACITY * me, CAPACITY)],
            )

        step = piece // CAPACITY
        for b in range(2):
            near_product(cast_ref, b)
        near_push(1, 1 + 2 * step)
        settle(up_recv.at[trip, pl.ds(0, devices - 1)], stage)

        def gather_parent(q):
            total = up_recv[trip, CHILDREN * q].astype(F32)
            for i in range(1, CHILDREN):
                total = total + up_recv[trip, CHILDREN * q + i].astype(F32)
            table_ref[level * parents + q] = total.astype(BF16)

        loop(parents, 8, gather_parent)
        mine = table_ref.at[pl.ds(level * parents, parents)]
        for i in range(1, CHILDREN):
            push(mine, mine, stage + 1, leaf * levels + (level + i) % levels)
        for b in range(2, CAPACITY):
            near_product(cast_ref, b)
        near_push(1 + 2 * step, SPLIT)
        if first:
            label_recv[pl.ds(me, 1)] = label_send[pl.ds(me, 1)]
            push_all(1, devices, 9, lambda e: label_send.at[e], label_recv.at[me])

            def fuse(c):
                value = jnp.dot(
                    basis_ref[c], transfer_ref[c], preferred_element_type=F32
                ).astype(BF16)
                product_ref[c] = value
                turned_ref[c] = value.T

            loop(clusters, 8, fuse)
            load_far.wait()
        settle(table_ref.at[pl.ds(0, (levels - 1) * parents)], stage + 1)

        def parent_of(j):
            return (leaf + 13 * j) % leaves

        group = BLOCK // levels

        def translate(block):
            values = []
            for u in range(group):
                q = parent_of(1 + block * group + u)
                picked = jnp.concatenate(
                    [table_ref[far_ref[k, q]] for k in range(partners)], axis=1
                )
                mats = far_w[pl.ds(partners * q, partners)].reshape(partners * lanes, lanes)
                values.append(jnp.dot(picked, mats, preferred_element_type=F32).astype(BF16))
            return values

        def keep(block, values):
            for u in range(group):
                down_send[trip, parent_of(1 + block * group + u)] = values[u]

        def send_down(block, last):
            for u in range(group):
                q = parent_of(1 + block * group + u)
                for i in range(1 if last and u == group - 1 else 0, levels):
                    other = q * levels + (level + i) % levels
                    push(down_send.at[trip, q], down_recv.at[me], stage + 2, other)

        keep(0, translate(0))

        def down(block, carry):
            values = translate(block)
            send_down(block - 1, False)
            keep(block, values)
            return carry

        lax.fori_loop(1, blocks, down, 0)
        send_down(blocks - 1, True)
        down_recv[me] = down_send[trip, leaf]
        near_push(SPLIT, devices)
        for k in range(CAPACITY):
            near_recv[CAPACITY * me + k] = part_ref[slot_of[k, me]].astype(BF16)
        if first:
            settle(label_recv.at[pl.ds(0, devices - 1)], 9)
            land_tables(
                label_recv[...].reshape(devices, lanes).astype(jnp.int32), land_rows
            )
            move_land = pltpu.make_async_copy(land_rows, land_of, table_sem.at[1])
            move_land.start()
            move_land.wait()
        settle(down_recv.at[pl.ds(0, devices - 1)], stage + 2)

        def spread(c):
            field_ref[c] = jnp.dot(
                down_recv[slot_of[CAPACITY, c]], turned_ref[c], preferred_element_type=F32
            )

        loop(clusters, 32, spread)
        settle(near_recv.at[pl.ds(0, CAPACITY * (devices - 1))], stage + 3)

        for b in range(CAPACITY):

            def land(block, total):
                for u in range(8):
                    i = block * 8 + u
                    total = total * land_of[CAPACITY + b, i].astype(F32) + near_recv[
                        land_of[b, i]
                    ].astype(F32)
                    run_ref[b * devices + i] = total
                return total

            total = lax.fori_loop(0, devices // 8, land, zero if b == 0 else total)

        def finish(block, sums):
            sums = list(sums)
            for u in range(8):
                c = block * 8 + u
                where = pl.ds(pl.multiple_of(c * lanes, lanes), lanes)
                value = field_ref[c] + run_ref[land_of[2 * CAPACITY, c]]
                x = x_ref[:, where]
                if first:
                    value = value * SCALE
                    z_ref[:, where] = value
                    cast_two[c] = value.astype(BF16)
                    terms = ((x, x), (x, value), (value, value))
                else:
                    u_ref[:, where] = value
                    terms = ((x, value), (z_ref[:, where], value), (value, value))
                for k, (p, q) in enumerate(terms):
                    sums[k] = sums[k] + p * q
            return tuple(sums)

        dots += lax.fori_loop(0, clusters // 8, finish, (zero,) * 3)
        store = pltpu.make_async_copy(
            z_ref if first else u_ref, z_hbm if first else u_hbm, table_sem.at[2 + trip]
        )
        store.start()
        sent.append(store)

    lane = lax.broadcasted_iota(jnp.int32, (systems, lanes), 1)
    row = lax.broadcasted_iota(jnp.int32, (systems, lanes), 0)
    packed = zero
    for k, total in enumerate(dots):
        packed = jnp.where(
            lane == row + k * systems, jnp.sum(total, axis=1, keepdims=True), packed
        )
    packed = jnp.sum(packed, axis=0, keepdims=True)
    teams = devices // TEAM
    team, member = me // TEAM, me % TEAM
    dot_send[0] = packed
    dot_recv[pl.ds(member, 1)] = packed[None]
    for i in range(1, TEAM):
        push(dot_send.at[0], dot_recv.at[member], 8, team * TEAM + (member + i) % TEAM)
    settle(dot_recv.at[pl.ds(0, TEAM - 1)], 8)
    packed = jnp.sum(dot_recv[pl.ds(0, TEAM)], axis=0)
    dot_send[1] = packed
    dot_recv[pl.ds(TEAM + team, 1)] = packed[None]
    for i in range(1, teams):
        push(dot_send.at[1], dot_recv.at[TEAM + team], 10, (me + TEAM * i) % devices)
    settle(dot_recv.at[pl.ds(TEAM, teams - 1)], 10)
    packed = jnp.sum(dot_recv[pl.ds(TEAM, teams)], axis=0)
    gathered = jnp.broadcast_to(packed, (systems, lanes))
    scalars = combine(
        [
            jnp.sum(jnp.where(lane == row + k * systems, gathered, 0.0), axis=1, keepdims=True)
            for k in range(len(dots))
        ]
    )
    for k, value in enumerate(scalars):
        coef_ref[k] = jnp.broadcast_to(value, (systems, lanes))
    for copy in sent:
        copy.wait()


def finish(coef_ref, x_ref, z_ref, u_ref, solved_ref, left_ref):
    first_x, first_z, second_x, second_z, second_u = (coef_ref[k] for k in range(5))
    lanes = coef_ref.shape[2]
    for c in range(x_ref.shape[1] // lanes):
        where = pl.ds(c * lanes, lanes)
        x, z, u = x_ref[:, where], z_ref[:, where], u_ref[:, where]
        solved_ref[:, where] = first_x * x + first_z * z
        left_ref[:, where] = second_x * x + second_z * z + second_u * u


def local(
    right_side,
    basis,
    transfer,
    order,
    far_src,
    far_mats,
    near_target,
    near_dest,
    near_src,
    near_blocks,
):
    systems, panels = right_side.shape
    clusters, points, coeffs = basis.shape
    devices = lax.axis_size(AXES)
    pairs = near_target.shape[0]
    parents = clusters // CHILDREN
    slots = CAPACITY * devices
    smem = pl.BlockSpec(memory_space=pltpu.SMEM)
    hbm = pl.BlockSpec(memory_space=pltpu.HBM)
    vmem = pl.BlockSpec(memory_space=pltpu.VMEM)
    field = jax.ShapeDtypeStruct((systems, panels), F32)
    cell = (systems, points)
    image, second, coefs = pl.pallas_call(
        kernel,
        name="gmres",
        out_shape=(field, field, jax.ShapeDtypeStruct((5, systems, points), F32)),
        in_specs=[smem] * 3 + [vmem] * 3 + [hbm] * 5,
        out_specs=(hbm, hbm, vmem),
        scratch_shapes=[
            pltpu.VMEM((systems, panels), F32),
            pltpu.VMEM((systems, panels), F32),
            pltpu.VMEM((systems, panels), F32),
            pltpu.VMEM(basis.shape, BF16),
            pltpu.VMEM(transfer.shape, BF16),
            pltpu.VMEM(basis.shape, BF16),
            pltpu.VMEM(basis.shape, BF16),
            pltpu.VMEM((parents * far_src.shape[1], coeffs, coeffs), BF16),
            pltpu.VMEM(near_blocks.shape, BF16),
            pltpu.VMEM((pairs, *cell), F32),
            pltpu.VMEM((clusters, *cell), F32),
            pltpu.VMEM((slots + 8, *cell), F32),
            pltpu.VMEM((clusters, *cell), BF16),
            pltpu.VMEM((2, clusters, *cell), BF16),
            pltpu.VMEM((2, clusters, *cell), BF16),
            pltpu.VMEM((2, parents, *cell), BF16),
            pltpu.VMEM((2, slots, *cell), BF16),
            pltpu.VMEM((CHILDREN * parents, *cell), BF16),
            pltpu.VMEM((CHILDREN * parents, *cell), BF16),
            pltpu.VMEM((clusters, *cell), BF16),
            pltpu.VMEM((clusters, *cell), BF16),
            pltpu.VMEM((slots, *cell), BF16),
            pltpu.VMEM((slots, *cell), BF16),
            pltpu.VMEM((clusters, *cell), BF16),
            pltpu.VMEM((clusters, *cell), BF16),
            pltpu.VMEM((2, 1, points), F32),
            pltpu.VMEM((TEAM + devices // TEAM, 1, points), F32),
            pltpu.VMEM((devices, 1, points), F32),
            pltpu.VMEM((devices, 1, points), F32),
            pltpu.VMEM((8, devices), jnp.int32),
            pltpu.VMEM((16, devices), jnp.int32),
            pltpu.SMEM((8, devices), jnp.int32),
            pltpu.SMEM((16, devices), jnp.int32),
            pltpu.SemaphoreType.DMA((11,)),
            pltpu.SemaphoreType.DMA((4,)),
            pltpu.SemaphoreType.DMA((11, 2)),
        ],
        compiler_params=pltpu.CompilerParams(
            collective_id=0, has_side_effects=True, vmem_limit_bytes=60 << 20
        ),
    )(
        near_target,
        order.reshape(-1),
        far_src.T,
        near_dest.reshape(-1, points),
        near_src.reshape(-1, points),
        order,
        right_side,
        basis,
        transfer,
        far_mats.reshape(-1, coeffs, coeffs),
        near_blocks,
    )
    block = pl.BlockSpec((systems, panels // 2), lambda i: (0, i))
    return pl.pallas_call(
        finish,
        name="outputs",
        grid=(2,),
        out_shape=(field, field),
        in_specs=[pl.BlockSpec((5, systems, points), lambda i: (0, 0, 0))] + [block] * 3,
        out_specs=(block, block),
        compiler_params=pltpu.CompilerParams(vmem_limit_bytes=60 << 20),
    )(coefs, right_side, image, second)


def solution(mesh):
    placed = (
        P(None, AXES),
        P(AXES, None, None),
        P(AXES, None, None),
        P(AXES, None),
        P(AXES, None),
        P(AXES, None, None, None),
        P(AXES),
        P(AXES, None),
        P(AXES),
        P(AXES, None, None),
    )
    return jax.shard_map(
        local,
        mesh=mesh,
        in_specs=placed,
        out_specs=(P(None, AXES), P(None, AXES)),
        check_vma=False,
    )
```
